256 devices in a mesh: loop: 16 (over y_hi, x, core), stack: 16 (over y_lo, z).
Axes of the slice: x: 4, y: 4 (y_hi: 2, y_lo: 2; y = y_hi * 2 + y_lo), z: 8, core: 2. Of those that a mesh axis runs over, the one named last changes fastest.
Arguments:
- spectra: bfloat16 [512, 2, 32, 2048], P('stack', None, None, 'loop'), may hold values from -6 to 6
- channel_loc: int32 [2048], P('loop'), may hold values from 0 to 4095, as said below
- channel_valid: int32 [2048], P('loop'), may hold values 0 or 1
- bin_owner: int32 [128], replicated, may hold values from 0 to 15, as said below
Outputs:
- linear_stack: float32 [16, 16, 1024], P('stack', 'loop')
- phase_stack: float32 [16, 16, 1024], P('stack', 'loop')
The draws below stay inside these ranges and needn't reach their ends.
Inputs may be any that keep to these rules, and one draw needn't show every extreme that they name: `channel_loc`: strictly increasing along the channels; channel c lies at 2 c or 2 c + 1, the first at 0 and the last at 4095. `bin_owner`: at most 16 bins share an owner; some owner holds exactly 16.
All inputs are finite; a program needn't handle non-finite values. No bound on the sum of `channel_valid` on one device may be relied on, other than what follows from the above.
Results may differ from the reference program's by a relative error of at most 0.003.
Values may be sent and summed in bfloat16 or wider, within the bound.
No kernel may reach another device: no remote copies, remote signals or barrier semaphores. Data moves between devices by JAX's collectives and lax.ppermute only.
A program may use at most 64 MiB of HBM per device.

```python
import math
import jax
import jax.numpy as jnp
from jax import lax

NFREQ = 512
SEG = 32
BIN_DEV = 8
NCH = 2048
NBIN = 128
BCAP = 16


def draw_channel_loc(key, part):
    positions = jnp.arange(NCH, dtype=jnp.int32)
    jitter = jax.random.randint(key, (NCH,), 0, 2, dtype=jnp.int32)
    jitter = jnp.where(positions == 0, 0, jnp.where(positions == NCH - 1, 1, jitter))
    return (2 * positions + jitter).astype(jnp.int32)


def draw_bin_owner(key, part):
    owner_count = NBIN // BIN_DEV
    key_full = jax.random.fold_in(key, 11)
    key_order = jax.random.fold_in(key, 12)
    key_slots = jax.random.fold_in(key, 13)
    full_owner = jax.random.randint(key_full, (), 0, owner_count, dtype=jnp.int32)
    bin_order = jax.random.permutation(key_order, NBIN).astype(jnp.int32)
    other_slots = jax.random.permutation(key_slots, (owner_count - 1) * BCAP).astype(jnp.int32)
    others = other_slots[:NBIN - BCAP] // BCAP
    others = others + (others >= full_owner).astype(jnp.int32)
    in_order = jnp.concatenate([jnp.full((BCAP,), full_owner, jnp.int32), others])
    return jnp.zeros((NBIN,), jnp.int32).at[bin_order].set(in_order)


def place_ends(drawn, rng, low, top_value):
    dims = drawn.shape
    index_at = [jax.random.randint(jax.random.fold_in(rng, axis), (), 0, dims[axis]) for axis in range(len(dims))]
    drawn = drawn.at[tuple(index_at)].set(low)
    longest = dims.index(max(dims))
    index_at[longest] = (index_at[longest] + 1) % dims[longest]
    return drawn.at[tuple(index_at)].set(top_value)


def shard_levels(stream_key, extent, shards, low, high):
    def one(dim, blocks):
        draws = jax.random.uniform(jax.random.fold_in(jax.random.fold_in(stream_key, 6), dim), (blocks,), jnp.float32, low / len(shards), high / len(shards))
        return jnp.repeat(jnp.exp(draws), extent[dim] // blocks).reshape((-1,) + (1,) * (len(extent) - dim - 1))

    level = one(*shards[0])
    for cut in shards[1:]:
        level = level * one(*cut)
    return level


def bell_draw(key, extent, width, most, cuts=(), kind=jnp.bfloat16):
    level = shard_levels(key, extent, cuts, -0.22, 0.18) if cuts else 1.0
    array = jax.random.normal(key, extent, jnp.float32) * width * level
    return jnp.minimum(jnp.maximum(array, -most), most).astype(kind)


def setup_inputs(seed: int = 0) -> dict:
    seeds = jax.random.split(jax.random.key(seed), 5)
    return {
        "spectra": bell_draw(seeds[0], (NFREQ, 2, SEG, NCH), 1.0, 6.0, ((0, 16), (3, 16))),
        "channel_loc": draw_channel_loc(jax.random.fold_in(seeds[4], 71), 0),
        "channel_valid": place_ends((jax.random.randint(seeds[2], (NCH,), 0, 8) < 7).astype(jnp.int32), jax.random.fold_in(seeds[2], 1), 0, 1),
        "bin_owner": draw_bin_owner(jax.random.fold_in(seeds[4], 71), 0),
    }


def lag_matrix(freq_count):
    freq_ids = jnp.arange(freq_count, dtype=jnp.int32)
    lag_ids = jnp.arange(2 * freq_count, dtype=jnp.int32) - freq_count
    turn_count = freq_ids[:, None] * lag_ids[None, :] % (2 * freq_count)
    phase_angle = turn_count.astype(jnp.float32) * (math.pi / freq_count)
    bin_weight = jnp.where(freq_ids == 0, 1.0, 2.0).astype(jnp.float32)[:, None]
    return jnp.concatenate([bin_weight * jnp.cos(phase_angle), -bin_weight * jnp.sin(phase_angle)], 0)

def normalize(series):
    return series / jnp.sqrt(lax.optimization_barrier(jnp.mean(series * series, axis=-1, keepdims=True)) + 1e-06)

def finish(linear_re, linear_im, phase_re, phase_im):
    coherence = phase_re * phase_re + phase_im * phase_im
    matrix = lag_matrix(linear_re.shape[1])
    linear = jnp.dot(jnp.concatenate([linear_re, linear_im], 1), matrix, precision=lax.Precision.HIGHEST)
    weighted = jnp.dot(jnp.concatenate([linear_re * coherence, linear_im * coherence], 1), matrix, precision=lax.Precision.HIGHEST)
    return (normalize(linear), normalize(weighted))

def reference(spectra, channel_loc, channel_valid, bin_owner):
    freq_count = spectra.shape[0]
    chan_count = spectra.shape[3]
    bin_count = bin_owner.shape[0]
    bin_width = 2 * chan_count // bin_count
    values_f = spectra.astype(jnp.float32)
    left_side = jnp.stack([values_f, jnp.stack([values_f[:, 1], -values_f[:, 0]], 1)], 1)
    valid_f = channel_valid.astype(jnp.float32)
    labels = jnp.arange(bin_count, dtype=jnp.int32)
    row_count = 16

    def add_block(running, block_index):
        first_row = (block_index * row_count).astype(jnp.int32)
        row_block = lax.dynamic_slice_in_dim(left_side, first_row, row_count, 4)
        products = jnp.einsum('fkpsa,fpsb->fkab', row_block, values_f, precision=lax.Precision.HIGHEST)
        real_part = products[:, 0]
        imag_part = products[:, 1]
        magnitude = jnp.maximum(jnp.sqrt(real_part * real_part + imag_part * imag_part), 1.0)
        components = jnp.stack([real_part, imag_part, real_part / magnitude, imag_part / magnitude], 1).astype(jnp.bfloat16)
        components = lax.optimization_barrier(components).astype(jnp.float32).reshape(freq_count * 4, row_count * chan_count)
        row_loc = lax.dynamic_slice_in_dim(channel_loc, first_row, row_count)
        row_valid = lax.dynamic_slice_in_dim(valid_f, first_row, row_count)
        loc_gap = channel_loc[None, :] - row_loc[:, None]
        weight = jnp.where(loc_gap > 0, row_valid[:, None] * valid_f[None, :], 0.0)
        pair_bin = jnp.where(loc_gap > 0, loc_gap // bin_width, 0)
        onehot = jnp.where(pair_bin[:, :, None] == labels, weight[:, :, None], 0.0).reshape(row_count * chan_count, bin_count)
        return (running + jnp.dot(components, onehot, precision=lax.Precision.HIGHEST), None)
    start_sum = jnp.zeros((freq_count * 4, bin_count), jnp.float32)
    running, _ = lax.scan(add_block, start_sum, jnp.arange(chan_count // row_count, dtype=jnp.int32))
    bin_sums = running.reshape(freq_count, 4, bin_count)
    linear, weighted = finish(bin_sums[:, 0].T, bin_sums[:, 1].T, bin_sums[:, 2].T, bin_sums[:, 3].T)
    same_owner = bin_owner[:, None] == bin_owner[None, :]
    earlier = labels[None, :] < labels[:, None]
    slot_rank = lax.optimization_barrier(jnp.sum((same_owner & earlier).astype(jnp.int32), axis=1))
    owner_count = bin_count // BIN_DEV
    blank = jnp.zeros((owner_count, BCAP, 2 * freq_count), jnp.float32)
    return (blank.at[bin_owner, slot_rank].set(linear), blank.at[bin_owner, slot_rank].set(weighted))
```

```python
import math

import jax
import jax.numpy as jnp
from jax import lax
from jax.experimental import pallas as pl
from jax.experimental.pallas import tpu as pltpu
from jax.sharding import PartitionSpec as P

BCAP = 16
F32 = jnp.float32
BF16 = jnp.bfloat16


def iota(shape, dim):
    return lax.broadcasted_iota(jnp.int32, shape, dim)


def dot_nt(a, b):
    return lax.dot_general(a, b, (((1,), (1,)), ((), ())), preferred_element_type=F32)


def dot_nn(a, b):
    return lax.dot_general(a, b, (((1,), (0,)), ((), ())), preferred_element_type=F32)


def pack_kernel(loc_ref, valid_ref, x_ref, o_ref):
    row = iota((128, 128), 0)
    col = iota((128, 128), 1)
    valid = jnp.broadcast_to(valid_ref[...].astype(F32), (128, 128))
    pick = jnp.where(col == 16 * (row % 8) + row // 8, valid, 0.0).astype(BF16)
    jit = jnp.broadcast_to((loc_ref[...] & 1).astype(F32), (16, 128))
    jit = jnp.where(iota((16, 128), 1) % 16 == iota((16, 128), 0), jit, 0.0).astype(BF16)
    spread = jnp.where(col == row // 16, 1.0, 0.0).astype(BF16)
    bits = dot_nn(jit, spread).astype(BF16)
    for g in range(x_ref.shape[0]):
        o_ref[g, 0:128] = dot_nt(pick, x_ref[g]).astype(BF16)
        o_ref[g, 128:144] = bits


def pack(channel_loc, channel_valid, blocks):
    count = blocks.shape[0]
    step = 4
    return pl.pallas_call(
        pack_kernel,
        grid=(count // step,),
        in_specs=[
            pl.BlockSpec((1, 128), lambda i: (0, 0)),
            pl.BlockSpec((1, 128), lambda i: (0, 0)),
            pl.BlockSpec((step, 128, 128), lambda i: (i, 0, 0)),
        ],
        out_specs=pl.BlockSpec((step, 144, 128), lambda i: (i, 0, 0)),
        out_shape=jax.ShapeDtypeStruct((count, 144, 128), BF16),
        name="pack",
    )(channel_loc.reshape(1, 128), channel_valid.reshape(1, 128), blocks)


def split3(x):
    hi = x.astype(BF16)
    rest = x - hi.astype(F32)
    mid = rest.astype(BF16)
    low = (rest - mid.astype(F32)).astype(BF16)
    return hi, mid, low


def skew_sum(x):
    total = x[0:8]
    for g in range(1, 16):
        total = total + pltpu.roll(x[8 * g : 8 * g + 8], 128 - 8 * g, 1)
    out = total[0:1]
    for s in range(1, 8):
        out = out + pltpu.roll(total[s : s + 1], 128 - s, 1)
    return out


CHUNK = 64
NCHUNK = 128 // CHUNK


def main_kernel(owner_row_ref, owner_col_ref, y_ref, o_ref, x_s, w_s, lin_s, acc_s, bits_s, pw_s):
    lane = iota((128, 128), 1)
    row = iota((128, 128), 0)
    sign = jnp.where(row // 32 % 2 == 1, 1.0, -1.0)
    swap = jnp.where(row == jnp.where(lane // 32 % 2 == 0, lane + 32, lane - 32), sign, 0.0).astype(BF16)

    bits = jnp.zeros((16, 128), F32)
    for g in range(16):
        piece = y_ref[g, 128:144, :].astype(F32)
        bits = bits + (pltpu.roll(piece, 8 * g, 1) if g else piece)
    bits_s[...] = bits
    bits_t = jnp.transpose(jnp.concatenate([bits, jnp.zeros((112, 128), F32)], 0))

    suffix = jnp.zeros((128, 128), F32)
    for r in reversed(range(16)):
        x = y_ref[:, 8 * r : 8 * r + 8, :].astype(F32).reshape(128, 128)
        xb = x.astype(BF16)
        for c in range(NCHUNK):
            x_s[c, CHUNK * r : CHUNK * r + CHUNK, :] = xb[CHUNK * c : CHUNK * c + CHUNK]
        xs = dot_nn(xb, swap)
        for f in range(2):
            mine = lane // 64 == f
            w_s[f, r, 0:128, :] = jnp.where(mine, x, 0.0).astype(BF16)
            w_s[f, r, 128:256, :] = jnp.where(mine, xs, 0.0).astype(BF16)
        hi = suffix.astype(BF16)
        lin_s[r, :, 0:128] = hi
        lin_s[r, :, 128:256] = (suffix - hi.astype(F32)).astype(BF16)
        suffix = suffix + x

    keep_low = row > lane
    keep_diag = row >= lane

    def one_freq(f, carry):
        lin = jnp.zeros((128, 256), F32)
        lin_same = jnp.zeros((128, 256), F32)
        lin_jit = jnp.zeros((128, 256), F32)
        acc_s[...] = jnp.zeros(acc_s.shape, F32)
        for r in range(16):
            w = w_s[f, r]
            lin = lin + dot_nt(lin_s[r], jnp.concatenate([w, w], 1))
            jit_lane = jnp.broadcast_to(bits_s[r : r + 1, :], (CHUNK, 128))
            for c in range(NCHUNK):
                rows = slice(CHUNK * c, CHUNK * c + CHUNK)
                prod = dot_nt(x_s[c, CHUNK * r :, :], w)
                acc_re = None
                for u in range(r, 16):
                    at = CHUNK * (u - r)
                    re = prod[at : at + CHUNK, 0:128]
                    im = prod[at : at + CHUNK, 128:256]
                    gain = lax.rsqrt(jnp.maximum(re * re + im * im, 1.0))
                    pr = re * gain
                    pi = im * gain
                    if u == r:
                        mask = jit_lane * (1.0 - jnp.broadcast_to(bits_t[rows, r : r + 1], (CHUNK, 128)))
                        acc_s[1, rows, 0:128] += pr
                        acc_s[1, rows, 128:256] += pi
                        acc_s[2, rows, 0:128] += pr * mask
                        acc_s[2, rows, 128:256] += pi * mask
                        acc_s[3, rows, 0:128] += re
                        acc_s[3, rows, 128:256] += im
                        acc_s[4, rows, 0:128] += re * mask
                        acc_s[4, rows, 128:256] += im * mask
                    elif acc_re is None:
                        acc_re, acc_im = pr, pi
                    else:
                        acc_re = acc_re + pr
                        acc_im = acc_im + pi
                if acc_re is not None:
                    acc_s[0, rows, 0:128] += acc_re
                    acc_s[0, rows, 128:256] += acc_im
        for part in range(4):
            cols = slice(128 * (part % 2), 128 * (part % 2) + 128)
            conj = 1.0 if part % 2 == 0 else -1.0
            if part < 2:
                full, same, jit = lin[:, cols], acc_s[3, :, cols], acc_s[4, :, cols]
            else:
                full, same, jit = acc_s[0, :, cols], acc_s[1, :, cols], acc_s[2, :, cols]
            low = jnp.where(keep_diag, full, 0.0) + jnp.where(keep_low, same - jit, 0.0)
            up = jnp.where(keep_diag, 0.0, full * conj)
            up = up + jnp.transpose(jnp.where(keep_low, jit, 0.0))
            pw_s[f, part : part + 1, 0:128] = skew_sum(low)
            pw_s[f, part : part + 1, 128:256] = skew_sum(up)
        return carry

    pw_s[...] = jnp.zeros(pw_s.shape, F32)
    lax.fori_loop(0, 2, one_freq, 0)

    owner_row = jnp.broadcast_to(owner_row_ref[...], (128, 128))
    owner_col = jnp.broadcast_to(owner_col_ref[...], (128, 128))
    before = jnp.where((owner_row == owner_col) & (lane < row), 1.0, 0.0)
    rank = jnp.sum(before, 1, keepdims=True).astype(jnp.int32)
    slot = jnp.broadcast_to(16 * owner_col_ref[...] + rank, (128, 256))
    place = jnp.where(slot == iota((128, 256), 1), 1.0, 0.0)
    low_pick = jnp.where((lane + row) % 128 == 0, 1.0, 0.0).astype(BF16)
    up_pick = jnp.where(row == lane + 1, 1.0, 0.0).astype(BF16)
    unpick = jnp.concatenate([low_pick, up_pick], 0)
    place_b = place.astype(BF16)
    gather = dot_nn(unpick, place_b).astype(BF16)
    hi, mid, low = split3(pw_s[...].reshape(16, 256))
    sums = dot_nn(hi, gather) + dot_nn(mid, gather) + dot_nn(low, gather)
    out = []
    for f in range(2):
        part = [sums[8 * f + p : 8 * f + p + 1] for p in range(4)]
        power = part[2] * part[2] + part[3] * part[3]
        out += [part[0], part[1], part[0] * power, part[1] * power]
    o_ref[...] = jnp.concatenate(out, 0)


def bin_sums(bin_owner, received):
    return pl.pallas_call(
        main_kernel,
        out_shape=jax.ShapeDtypeStruct((8, 256), F32),
        scratch_shapes=[
            pltpu.VMEM((NCHUNK, 16 * CHUNK, 128), BF16),
            pltpu.VMEM((2, 16, 256, 128), BF16),
            pltpu.VMEM((16, 128, 256), BF16),
            pltpu.VMEM((5, 128, 256), F32),
            pltpu.VMEM((16, 128), F32),
            pltpu.VMEM((2, 8, 256), F32),
        ],
        name="bin_sums",
    )(bin_owner.reshape(1, 128), bin_owner.reshape(128, 1), received)


def on_device(spectra, channel_loc, channel_valid, bin_owner):
    groups = lax.axis_size("loop")
    owners = lax.axis_size("stack")
    blocks = spectra.reshape(groups, 128, 128)
    packed = pack(channel_loc, channel_valid, blocks)
    received = lax.all_to_all(packed, "loop", split_axis=0, concat_axis=0, tiled=True)
    sums = bin_sums(bin_owner, received)
    by_rank = sums.reshape(8, owners, BCAP).transpose(2, 1, 0).reshape(BCAP, owners * 8)
    by_rank = lax.all_to_all(by_rank, "loop", split_axis=0, concat_axis=0, tiled=True)
    by_owner = by_rank.reshape(groups, owners, 8).transpose(1, 0, 2).reshape(owners, groups * 8)
    mine = lax.all_to_all(by_owner, "stack", split_axis=0, concat_axis=0, tiled=True)
    mine = mine.reshape(owners * groups * 2, 4).T
    return finish(mine)


def finish(mine):
    return finish_plain(mine)


def lag_matrix(freq_count):
    freq_ids = jnp.arange(freq_count, dtype=jnp.int32)
    lag_ids = jnp.arange(2 * freq_count, dtype=jnp.int32) - freq_count
    turn_count = freq_ids[:, None] * lag_ids[None, :] % (2 * freq_count)
    phase_angle = turn_count.astype(jnp.float32) * (math.pi / freq_count)
    bin_weight = jnp.where(freq_ids == 0, 1.0, 2.0).astype(jnp.float32)[:, None]
    return jnp.concatenate(
        [bin_weight * jnp.cos(phase_angle), -bin_weight * jnp.sin(phase_angle)], 0
    )


def normalize(series):
    return series / jnp.sqrt(jnp.mean(series * series, axis=-1, keepdims=True) + 1e-06)


def finish_plain(mine):
    both = mine.reshape(2, -1)
    series = jnp.dot(both, lag_matrix(mine.shape[1]), precision=lax.Precision.HIGHEST)
    series = normalize(series)
    return series[0].reshape(1, 1, -1), series[1].reshape(1, 1, -1)


def solution(mesh):
    in_specs = (P("stack", None, None, "loop"), P("loop"), P("loop"), P())
    out_specs = (P("stack", "loop", None), P("stack", "loop", None))
    return jax.shard_map(
        on_device, mesh=mesh, in_specs=in_specs, out_specs=out_specs, check_vma=False
    )
```

```python
import jax
import jax.numpy as jnp
import numpy as np
from jax import lax
from jax.experimental import pallas as pl
from jax.experimental.pallas import tpu as pltpu
from jax.sharding import PartitionSpec as P

F32 = jnp.float32
BF16 = jnp.bfloat16


def iota(shape, dim):
    return lax.broadcasted_iota(jnp.int32, shape, dim)


def dot_nt(a, b):
    return lax.dot_general(a, b, (((1,), (1,)), ((), ())), preferred_element_type=F32)


def dot_nn(a, b):
    return lax.dot_general(a, b, (((1,), (0,)), ((), ())), preferred_element_type=F32)


def pack_kernel(loc_ref, valid_ref, x_ref, o_ref):
    row = iota((128, 128), 0)
    col = iota((128, 128), 1)
    valid = jnp.broadcast_to(valid_ref[...].astype(F32), (128, 128))
    pick = jnp.where(col == 16 * (row % 8) + row // 8, valid, 0.0).astype(BF16)
    jit = jnp.broadcast_to((loc_ref[...] & 1).astype(F32), (16, 128))
    jit = jnp.where(iota((16, 128), 1) % 16 == iota((16, 128), 0), jit, 0.0).astype(BF16)
    spread = jnp.where(col == row // 16, 1.0, 0.0).astype(BF16)
    bits = dot_nn(jit, spread).astype(BF16)
    for g in range(x_ref.shape[0]):
        o_ref[g, 0:128] = dot_nt(pick, x_ref[g]).astype(BF16)
        o_ref[g, 128:144] = bits


def pack(channel_loc, channel_valid, blocks):
    count = blocks.shape[0]
    step = 4
    return pl.pallas_call(
        pack_kernel,
        grid=(count // step,),
        in_specs=[
            pl.BlockSpec((1, 128), lambda i: (0, 0)),
            pl.BlockSpec((1, 128), lambda i: (0, 0)),
            pl.BlockSpec((step, 128, 128), lambda i: (i, 0, 0)),
        ],
        out_specs=pl.BlockSpec((step, 144, 128), lambda i: (i, 0, 0)),
        out_shape=jax.ShapeDtypeStruct((count, 144, 128), BF16),
        name="pack",
    )(channel_loc.reshape(1, 128), channel_valid.reshape(1, 128), blocks)


def split3(x):
    hi = x.astype(BF16)
    rest = x - hi.astype(F32)
    mid = rest.astype(BF16)
    low = (rest - mid.astype(F32)).astype(BF16)
    return hi, mid, low


def skew_sum(x):
    total = x[0:8]
    for g in range(1, 16):
        total = total + pltpu.roll(x[8 * g : 8 * g + 8], 128 - 8 * g, 1)
    out = total[0:1]
    for s in range(1, 8):
        out = out + pltpu.roll(total[s : s + 1], 128 - s, 1)
    return out


def exact_dot(x, picks):
    hi, mid, rest = split3(x)
    return dot_nn(hi, picks) + dot_nn(mid, picks) + dot_nn(rest, picks)


CHUNK = 64
NCHUNK = 128 // CHUNK


def main_kernel(owner_row_ref, y_ref, o_ref, x_s, w_s, lin_s, acc_s, bits_s, pw_s):
    lane = iota((128, 128), 1)
    row = iota((128, 128), 0)
    sign = jnp.where(row // 32 % 2 == 1, 1.0, -1.0)
    swap = jnp.where(row == jnp.where(lane // 32 % 2 == 0, lane + 32, lane - 32), sign, 0.0).astype(BF16)

    bits = jnp.zeros((16, 128), F32)
    for g in range(16):
        piece = y_ref[g, 128:144, :].astype(F32)
        bits = bits + (pltpu.roll(piece, 8 * g, 1) if g else piece)
    bits_s[...] = bits
    bits_t = jnp.transpose(jnp.concatenate([bits, jnp.zeros((112, 128), F32)], 0))

    suffix = jnp.zeros((128, 128), F32)
    for r in reversed(range(16)):
        x = y_ref[:, 8 * r : 8 * r + 8, :].astype(F32).reshape(128, 128)
        xb = x.astype(BF16)
        for c in range(NCHUNK):
            x_s[c, CHUNK * r : CHUNK * r + CHUNK, :] = xb[CHUNK * c : CHUNK * c + CHUNK]
        xs = dot_nn(xb, swap)
        for f in range(2):
            mine = lane // 64 == f
            w_s[f, r, 0:128, :] = jnp.where(mine, x, 0.0).astype(BF16)
            w_s[f, r, 128:256, :] = jnp.where(mine, xs, 0.0).astype(BF16)
        hi = suffix.astype(BF16)
        lin_s[r, :, 0:128] = hi
        lin_s[r, :, 128:256] = (suffix - hi.astype(F32)).astype(BF16)
        suffix = suffix + x

    keep_low = row > lane
    keep_diag = row >= lane

    def one_freq(f, carry):
        lin = jnp.zeros((128, 256), F32)
        lin_same = jnp.zeros((128, 256), F32)
        lin_jit = jnp.zeros((128, 256), F32)
        acc_s[...] = jnp.zeros(acc_s.shape, F32)
        for r in range(16):
            w = w_s[f, r]
            lin = lin + dot_nt(lin_s[r], jnp.concatenate([w, w], 1))
            jit_lane = jnp.broadcast_to(bits_s[r : r + 1, :], (CHUNK, 128))
            for c in range(NCHUNK):
                rows = slice(CHUNK * c, CHUNK * c + CHUNK)
                prod = dot_nt(x_s[c, CHUNK * r :, :], w)
                acc_re = None
                for u in range(r, 16):
                    at = CHUNK * (u - r)
                    re = prod[at : at + CHUNK, 0:128]
                    im = prod[at : at + CHUNK, 128:256]
                    gain = lax.rsqrt(jnp.maximum(re * re + im * im, 1.0))
                    pr = re * gain
                    pi = im * gain
                    if u == r:
                        mask = jit_lane * (1.0 - jnp.broadcast_to(bits_t[rows, r : r + 1], (CHUNK, 128)))
                        acc_s[1, rows, 0:128] += pr
                        acc_s[1, rows, 128:256] += pi
                        acc_s[2, rows, 0:128] += pr * mask
                        acc_s[2, rows, 128:256] += pi * mask
                        acc_s[3, rows, 0:128] += re
                        acc_s[3, rows, 128:256] += im
                        acc_s[4, rows, 0:128] += re * mask
                        acc_s[4, rows, 128:256] += im * mask
                    elif acc_re is None:
                        acc_re, acc_im = pr, pi
                    else:
                        acc_re = acc_re + pr
                        acc_im = acc_im + pi
                if acc_re is not None:
                    acc_s[0, rows, 0:128] += acc_re
                    acc_s[0, rows, 128:256] += acc_im
        for part in range(4):
            cols = slice(128 * (part % 2), 128 * (part % 2) + 128)
            conj = 1.0 if part % 2 == 0 else -1.0
            if part < 2:
                full, same, jit = lin[:, cols], acc_s[3, :, cols], acc_s[4, :, cols]
            else:
                full, same, jit = acc_s[0, :, cols], acc_s[1, :, cols], acc_s[2, :, cols]
            low = jnp.where(keep_diag, full, 0.0) + jnp.where(keep_low, same - jit, 0.0)
            up = jnp.where(keep_diag, 0.0, full * conj)
            up = up + jnp.transpose(jnp.where(keep_low, jit, 0.0))
            pw_s[f, part : part + 1, 0:128] = skew_sum(low)
            pw_s[f, part : part + 1, 128:256] = skew_sum(up)
        return carry

    pw_s[...] = jnp.zeros(pw_s.shape, F32)
    lax.fori_loop(0, 2, one_freq, 0)

    low_pick = jnp.where((lane + row) % 128 == 0, 1.0, 0.0)
    up_pick = jnp.where(row == lane + 1, 1.0, 0.0)
    unpick = jnp.concatenate([low_pick, up_pick], 0).astype(BF16)
    sums = exact_dot(pw_s[...].reshape(16, 256), unpick)
    out = []
    for f in range(2):
        part = [sums[8 * f + p : 8 * f + p + 1] for p in range(4)]
        power = part[2] * part[2] + part[3] * part[3]
        out += [part[0], part[1], part[0] * power, part[1] * power]
    owner_row = jnp.broadcast_to(owner_row_ref[...], (128, 128))
    earlier = (owner_row == jnp.transpose(owner_row)) & (row < lane)
    rank = jnp.sum(jnp.where(earlier, 1.0, 0.0), 0, keepdims=True).astype(jnp.int32)
    slot = 16 * owner_row_ref[...] + rank
    place = jnp.where(iota((256, 128), 0) == slot, 1.0, 0.0).astype(BF16)
    by_bin = jnp.transpose(jnp.concatenate(out + [jnp.zeros((120, 128), F32)], 0))
    hi, mid, rest = split3(by_bin)
    placed = dot_nn(place, hi) + dot_nn(place, mid) + dot_nn(place, rest)
    o_ref[...] = placed[:, 0:8]


def bin_sums(bin_owner, received):
    vmem = pl.BlockSpec(memory_space=pltpu.VMEM)
    return pl.pallas_call(
        main_kernel,
        in_specs=[vmem, vmem],
        out_specs=vmem,
        out_shape=jax.ShapeDtypeStruct((256, 8), F32),
        scratch_shapes=[
            pltpu.VMEM((NCHUNK, 16 * CHUNK, 128), BF16),
            pltpu.VMEM((2, 16, 256, 128), BF16),
            pltpu.VMEM((16, 128, 256), BF16),
            pltpu.VMEM((5, 128, 256), F32),
            pltpu.VMEM((16, 128), F32),
            pltpu.VMEM((2, 8, 256), F32),
        ],
        name="bin_sums",
    )(bin_owner.reshape(1, 128), received)


def lag_tables():
    lane = np.arange(128)
    f0 = lane // 8 * 2 + lane % 8 // 4
    imag = lane % 2
    weight = np.full((16, 128), 2.0) * np.where(f0 % 2, -1.0, 1.0)
    weight[0, f0 == 0] = 1.0
    turn0 = 2 * np.pi * (np.arange(32)[:, None] * np.arange(16) % 32) / 32
    first = np.concatenate([np.cos(turn0), np.sin(turn0)], 0)
    turn1 = 2 * np.pi * (np.arange(128)[:, None] * f0 % 1024) / 1024
    t1 = np.where(imag, -np.sin(turn1), np.cos(turn1))
    t2 = np.where(imag, -np.cos(turn1), -np.sin(turn1))
    turn2 = 2 * np.pi * (np.arange(8)[:, None] * f0 % 8) / 8
    which = [lane % 4 // 2 == 0, lane % 4 // 2 == 1]
    last = [np.concatenate([np.cos(turn2) * w, -np.sin(turn2) * w], 1) for w in which]
    return [np.asarray(t, np.float32) for t in (weight, first, np.stack([t1, t2]), np.concatenate(last, 0))]


def finish_kernel(x_ref, weight_ref, first_ref, twiddle_ref, last_ref, lin_ref, phase_ref):
    spread = jnp.where(iota((8, 128), 0) == iota((8, 128), 1) % 8, 1.0, 0.0).astype(BF16)
    wide = exact_dot(x_ref[...], spread)
    wide = jnp.where(iota((256, 128), 0) % 16 == iota((256, 128), 1) // 8, wide, 0.0)
    z = jnp.sum(wide.reshape(16, 16, 128), 1) * weight_ref[...]
    high = lax.Precision.HIGHEST
    v = jnp.dot(first_ref[...], z, precision=high, preferred_element_type=F32)
    g = jnp.concatenate([v[0:32]] * 4, 0)
    h = jnp.concatenate([v[32:64]] * 4, 0)
    t1 = twiddle_ref[0]
    t2 = twiddle_ref[1]
    q = jnp.concatenate([g * t1 + h * t2, h * t1 - g * t2], 1)
    series = lax.dot_general(
        last_ref[...], q, (((1,), (1,)), ((), ())), precision=high, preferred_element_type=F32
    )
    for i, o_ref in enumerate((lin_ref, phase_ref)):
        c = series[8 * i : 8 * i + 8]
        o_ref[...] = c / jnp.sqrt(jnp.sum(c * c) * (1.0 / 1024) + 1e-06)


def finish(mine):
    vmem = pl.BlockSpec(memory_space=pltpu.VMEM)
    return pl.pallas_call(
        finish_kernel,
        in_specs=[vmem] * 5,
        out_specs=[vmem] * 2,
        out_shape=[jax.ShapeDtypeStruct((8, 128), F32)] * 2,
        name="finish",
    )(mine, *[jnp.asarray(t) for t in lag_tables()])


def exchange(x, axis):
    return lax.all_to_all(x, axis, split_axis=0, concat_axis=0, tiled=True)


def on_device(spectra, channel_loc, channel_valid, bin_owner):
    blocks = spectra.reshape(lax.axis_size("loop"), 128, 128)
    received = exchange(pack(channel_loc, channel_valid, blocks), "loop")
    sums = bin_sums(bin_owner, received)
    linear, phase = finish(exchange(sums, ("stack", "loop")))
    return linear.reshape(1, 1, -1), phase.reshape(1, 1, -1)


def solution(mesh):
    in_specs = (P("stack", None, None, "loop"), P("loop"), P("loop"), P())
    out_specs = (P("stack", "loop", None), P("stack", "loop", None))
    return jax.shard_map(
        on_device, mesh=mesh, in_specs=in_specs, out_specs=out_specs, check_vma=False
    )
```

```python
import jax
import jax.numpy as jnp
import numpy as np
from jax import lax
from jax.experimental import pallas as pl
from jax.experimental.pallas import tpu as pltpu
from jax.sharding import PartitionSpec as P

F32 = jnp.float32
BF16 = jnp.bfloat16


def iota(shape, dim):
    return lax.broadcasted_iota(jnp.int32, shape, dim)


def dot_nt(a, b):
    return lax.dot_general(a, b, (((1,), (1,)), ((), ())), preferred_element_type=F32)


def dot_nn(a, b):
    return lax.dot_general(a, b, (((1,), (0,)), ((), ())), preferred_element_type=F32)


PIECES = 4


def pack_kernel(loc_ref, valid_ref, x_hbm, o_ref, x_ref, sems):
    count = x_ref.shape[0]
    size = count // PIECES
    copies = [
        pltpu.make_async_copy(x_hbm.at[pl.ds(i * size, size)], x_ref.at[pl.ds(i * size, size)], sems.at[i])
        for i in range(PIECES)
    ]
    for copy in copies:
        copy.start()
    row = iota((128, 128), 0)
    col = iota((128, 128), 1)
    valid = jnp.broadcast_to(valid_ref[...].astype(F32), (128, 128))
    pick = jnp.where(col == 16 * (row % 8) + row // 8, valid, 0.0).astype(BF16)
    jit = jnp.broadcast_to((loc_ref[...] & 1).astype(F32), (16, 128))
    jit = jnp.where(iota((16, 128), 1) // 16 == iota((16, 128), 0), jit, 0.0).astype(BF16)
    spread = jnp.where(col == row % 16, 1.0, 0.0).astype(BF16)
    bits = dot_nn(jit, spread)[0:8].astype(BF16)
    for i, copy in enumerate(copies):
        copy.wait()
        for g in range(i * size, (i + 1) * size):
            o_ref[g, 0:128] = dot_nt(pick, x_ref[g]).astype(BF16)
            o_ref[g, 128:136] = bits


def pack(channel_loc, channel_valid, blocks):
    count = blocks.shape[0]
    vmem = pl.BlockSpec(memory_space=pltpu.VMEM)
    return pl.pallas_call(
        pack_kernel,
        in_specs=[vmem, vmem, pl.BlockSpec(memory_space=pl.ANY)],
        out_specs=vmem,
        out_shape=pltpu.VMEM((count, 136, 128), BF16),
        scratch_shapes=[pltpu.VMEM((count, 128, 128), BF16), pltpu.SemaphoreType.DMA((PIECES,))],
        name="pack",
    )(channel_loc.reshape(1, 128), channel_valid.reshape(1, 128), blocks)


def split3(x):
    hi = x.astype(BF16)
    rest = x - hi.astype(F32)
    mid = rest.astype(BF16)
    low = (rest - mid.astype(F32)).astype(BF16)
    return hi, mid, low


def skew_sum(x):
    total = x[0:8]
    for g in range(1, 16):
        total = total + pltpu.roll(x[8 * g : 8 * g + 8], 128 - 8 * g, 1)
    out = total[0:1]
    for s in range(1, 8):
        out = out + pltpu.roll(total[s : s + 1], 128 - s, 1)
    return out


def exact_dot(x, picks):
    hi, mid, rest = split3(x)
    return dot_nn(hi, picks) + dot_nn(mid, picks) + dot_nn(rest, picks)


CHUNK = 32
NCHUNK = 128 // CHUNK


def main_kernel(owner_row_ref, y_ref, o_ref, x_s, w_s, lin_s, mask_s, lin_acc, acc_s, pw_s):
    lane = iota((128, 128), 1)
    row = iota((128, 128), 0)
    sign = jnp.where(row // 32 % 2 == 1, 1.0, -1.0)
    swap = jnp.where(row == jnp.where(lane // 32 % 2 == 0, lane + 32, lane - 32), sign, 0.0).astype(BF16)
    bits_t = y_ref[:, 128:136, :].astype(F32).reshape(128, 128)
    bits = jnp.transpose(bits_t)
    own = [jnp.where(lane // 64 == f, 1.0, 0.0).astype(BF16) for f in range(2)]

    edge = jnp.where(row > lane, 1.0, jnp.where(row < lane, 0.0, -1.0))
    suffix = jnp.zeros((128, 128), F32)
    for r in reversed(range(16)):
        late = jnp.broadcast_to(bits_t[:, r : r + 1], (128, 128))
        gap = late - jnp.broadcast_to(bits[r : r + 1, :], (128, 128))
        mask_s[r] = jnp.minimum(jnp.maximum(edge + gap, 0.0), 1.0)
        x = y_ref[:, 8 * r : 8 * r + 8, :].astype(F32).reshape(128, 128)
        xb = x.astype(BF16)
        w_s[r, 0:128, :] = xb
        w_s[r, 128:256, :] = dot_nn(xb, swap).astype(BF16)
        hi = suffix.astype(BF16)
        low = (suffix - hi.astype(F32)).astype(BF16)
        for f in range(2):
            mine = xb * own[f]
            for c in range(NCHUNK):
                x_s[f, c, CHUNK * r : CHUNK * r + CHUNK, :] = mine[CHUNK * c : CHUNK * c + CHUNK]
            lin_s[f, :, 256 * r : 256 * r + 128] = hi * own[f]
            lin_s[f, :, 256 * r + 128 : 256 * r + 256] = low * own[f]
        suffix = suffix + x

    acc_s[...] = jnp.zeros(acc_s.shape, F32)

    keep_diag = row >= lane

    def one_freq(f, carry):
        lin = jnp.zeros((128, 256), F32)
        lin_acc[...] = jnp.zeros(lin_acc.shape, F32)
        for r in range(16):
            w = w_s[r]
            lin = lin + dot_nt(lin_s[f, :, 256 * r : 256 * r + 256], jnp.concatenate([w, w], 1))
            for c in range(NCHUNK):
                rows = slice(CHUNK * c, CHUNK * c + CHUNK)
                prod = dot_nt(x_s[f, c, CHUNK * r :, :], w)
                mask = mask_s[r, rows]
                for u in range(r, 16):
                    at = CHUNK * (u - r)
                    re = prod[at : at + CHUNK, 0:128]
                    im = prod[at : at + CHUNK, 128:256]
                    gain = lax.rsqrt(jnp.maximum(re * re + im * im, 1.0))
                    if u == r:
                        lin_acc[rows, 0:128] += re * mask
                        lin_acc[rows, 128:256] += im * mask
                        gain = gain * mask
                        acc_re = re * gain
                        acc_im = im * gain
                    else:
                        acc_re = acc_re + re * gain
                        acc_im = acc_im + im * gain
                acc_s[f, rows, 0:128] += acc_re
                acc_s[f, rows, 128:256] += acc_im
        for part in range(4):
            cols = slice(128 * (part % 2), 128 * (part % 2) + 128)
            full = lin[:, cols] + lin_acc[:, cols] if part < 2 else acc_s[f, :, cols]
            low = skew_sum(jnp.where(keep_diag, full, 0.0))
            up = skew_sum(jnp.where(keep_diag, 0.0, full))
            pw_s[f, part : part + 1, 0:128] = low
            pw_s[f, part : part + 1, 128:256] = up if part % 2 == 0 else -up
        return carry

    pw_s[...] = jnp.zeros(pw_s.shape, F32)
    lax.fori_loop(0, 2, one_freq, 0)

    low_pick = jnp.where((lane + row) % 128 == 0, 1.0, 0.0)
    up_pick = jnp.where(row == lane + 1, 1.0, 0.0)
    unpick = jnp.concatenate([low_pick, up_pick], 0).astype(BF16)
    sums = exact_dot(pw_s[...].reshape(16, 256), unpick)
    out = []
    for f in range(2):
        part = [sums[8 * f + p : 8 * f + p + 1] for p in range(4)]
        power = part[2] * part[2] + part[3] * part[3]
        out += [part[0], part[1], part[0] * power, part[1] * power]
    owner_row = jnp.broadcast_to(owner_row_ref[...], (128, 128))
    earlier = (owner_row == jnp.transpose(owner_row)) & (row < lane)
    rank = jnp.sum(jnp.where(earlier, 1.0, 0.0), 0, keepdims=True).astype(jnp.int32)
    slot = 16 * owner_row_ref[...] + rank
    place = jnp.where(iota((256, 128), 0) == slot, 1.0, 0.0).astype(BF16)
    by_bin = jnp.transpose(jnp.concatenate(out + [jnp.zeros((120, 128), F32)], 0))
    hi, mid, rest = split3(by_bin)
    placed = dot_nn(place, hi) + dot_nn(place, mid) + dot_nn(place, rest)
    o_ref[...] = placed[:, 0:8]


def bin_sums(bin_owner, received):
    vmem = pl.BlockSpec(memory_space=pltpu.VMEM)
    return pl.pallas_call(
        main_kernel,
        in_specs=[vmem, vmem],
        out_specs=vmem,
        out_shape=pltpu.VMEM((256, 8), F32),
        scratch_shapes=[
            pltpu.VMEM((2, NCHUNK, 16 * CHUNK, 128), BF16),
            pltpu.VMEM((16, 256, 128), BF16),
            pltpu.VMEM((2, 128, 16 * 256), BF16),
            pltpu.VMEM((16, 128, 128), F32),
            pltpu.VMEM((128, 256), F32),
            pltpu.VMEM((2, 128, 256), F32),
            pltpu.VMEM((2, 8, 256), F32),
        ],
        name="bin_sums",
    )(bin_owner.reshape(1, 128), received)


def lag_tables():
    lane = np.arange(128)
    f0 = lane // 8 * 2 + lane % 8 // 4
    imag = lane % 2
    weight = np.full((16, 128), 2.0) * np.where(f0 % 2, -1.0, 1.0)
    weight[0, f0 == 0] = 1.0
    turn0 = 2 * np.pi * (np.arange(32)[:, None] * np.arange(16) % 32) / 32
    first = np.concatenate([np.cos(turn0), np.sin(turn0)], 0)
    turn1 = 2 * np.pi * (np.arange(128)[:, None] * f0 % 1024) / 1024
    t1 = np.where(imag, -np.sin(turn1), np.cos(turn1))
    t2 = np.where(imag, -np.cos(turn1), -np.sin(turn1))
    turn2 = 2 * np.pi * (np.arange(8)[:, None] * f0 % 8) / 8
    which = [lane % 4 // 2 == 0, lane % 4 // 2 == 1]
    last = [np.concatenate([np.cos(turn2) * w, -np.sin(turn2) * w], 1) for w in which]
    return [np.asarray(t, np.float32) for t in (weight, first, np.stack([t1, t2]), np.concatenate(last, 0))]


def finish_kernel(x_ref, weight_ref, first_ref, twiddle_ref, last_ref, lin_ref, phase_ref):
    spread = jnp.where(iota((8, 128), 0) == iota((8, 128), 1) % 8, 1.0, 0.0).astype(BF16)
    wide = exact_dot(x_ref[...], spread)
    wide = jnp.where(iota((256, 128), 0) % 16 == iota((256, 128), 1) // 8, wide, 0.0)
    z = jnp.sum(wide.reshape(16, 16, 128), 1) * weight_ref[...]
    high = lax.Precision.HIGHEST
    v = jnp.dot(first_ref[...], z, precision=high, preferred_element_type=F32)
    g = jnp.concatenate([v[0:32]] * 4, 0)
    h = jnp.concatenate([v[32:64]] * 4, 0)
    t1 = twiddle_ref[0]
    t2 = twiddle_ref[1]
    q = jnp.concatenate([g * t1 + h * t2, h * t1 - g * t2], 1)
    series = lax.dot_general(
        last_ref[...], q, (((1,), (1,)), ((), ())), precision=high, preferred_element_type=F32
    )
    for i, o_ref in enumerate((lin_ref, phase_ref)):
        c = series[8 * i : 8 * i + 8]
        o_ref[...] = c / jnp.sqrt(jnp.sum(c * c) * (1.0 / 1024) + 1e-06)


def finish(mine):
    vmem = pl.BlockSpec(memory_space=pltpu.VMEM)
    return pl.pallas_call(
        finish_kernel,
        in_specs=[vmem] * 5,
        out_specs=[vmem] * 2,
        out_shape=[jax.ShapeDtypeStruct((8, 128), F32)] * 2,
        name="finish",
    )(mine, *[in_vmem(jnp.asarray(t)) for t in lag_tables()])


def in_vmem(x):
    return pltpu.with_memory_space_constraint(x, pltpu.VMEM)


def exchange(x, axis):
    return lax.all_to_all(x, axis, split_axis=0, concat_axis=0, tiled=True)


def on_device(spectra, channel_loc, channel_valid, bin_owner):
    blocks = spectra.reshape(lax.axis_size("loop"), 128, 128)
    received = exchange(pack(channel_loc, channel_valid, blocks), "loop")
    received = in_vmem(received)
    sums = bin_sums(bin_owner, received)
    linear, phase = finish(in_vmem(exchange(sums, ("stack", "loop"))))
    return linear.reshape(1, 1, -1), phase.reshape(1, 1, -1)


def solution(mesh):
    in_specs = (P("stack", None, None, "loop"), P("loop"), P("loop"), P())
    out_specs = (P("stack", "loop", None), P("stack", "loop", None))
    return jax.shard_map(
        on_device, mesh=mesh, in_specs=in_specs, out_specs=out_specs, check_vma=False
    )
```

```python
import jax
import jax.numpy as jnp
import numpy as np
from jax import lax
from jax.experimental import pallas as pl
from jax.experimental.pallas import tpu as pltpu
from jax.sharding import PartitionSpec as P

F32 = jnp.float32
BF16 = jnp.bfloat16


def iota(shape, dim):
    return lax.broadcasted_iota(jnp.int32, shape, dim)


def dot_nt(a, b):
    return lax.dot_general(a, b, (((1,), (1,)), ((), ())), preferred_element_type=F32)


def dot_nn(a, b):
    return lax.dot_general(a, b, (((1,), (0,)), ((), ())), preferred_element_type=F32)


PIECES = 4


def pack_kernel(loc_hbm, valid_hbm, x_hbm, o_ref, loc_ref, valid_ref, x_ref, sems):
    count = x_ref.shape[0]
    size = count // PIECES
    copies = [
        pltpu.make_async_copy(x_hbm.at[pl.ds(i * size, size)], x_ref.at[pl.ds(i * size, size)], sems.at[i])
        for i in range(PIECES)
    ]
    small = [
        pltpu.make_async_copy(loc_hbm, loc_ref, sems.at[PIECES]),
        pltpu.make_async_copy(valid_hbm, valid_ref, sems.at[PIECES + 1]),
    ]
    for copy in small + copies:
        copy.start()
    for copy in small:
        copy.wait()
    row = iota((128, 128), 0)
    col = iota((128, 128), 1)
    valid = jnp.broadcast_to(valid_ref[...].astype(F32), (128, 128))
    pick = jnp.where(col == 16 * (row % 8) + row // 8, valid, 0.0).astype(BF16)
    jit = jnp.broadcast_to((loc_ref[...] & 1).astype(F32), (16, 128))
    jit = jnp.where(iota((16, 128), 1) // 16 == iota((16, 128), 0), jit, 0.0).astype(BF16)
    spread = jnp.where(col == row % 16, 1.0, 0.0).astype(BF16)
    bits = dot_nn(jit, spread)[0:8].astype(BF16)
    for i, copy in enumerate(copies):
        copy.wait()
        for g in range(i * size, (i + 1) * size):
            o_ref[g, 0:128] = dot_nt(pick, x_ref[g]).astype(BF16)
            o_ref[g, 128:136] = bits


def pack(channel_loc, channel_valid, blocks):
    count = blocks.shape[0]
    return pl.pallas_call(
        pack_kernel,
        in_specs=[pl.BlockSpec(memory_space=pl.ANY)] * 3,
        out_specs=pl.BlockSpec(memory_space=pltpu.VMEM),
        out_shape=pltpu.VMEM((count, 136, 128), BF16),
        scratch_shapes=[
            pltpu.VMEM((1, 128), jnp.int32),
            pltpu.VMEM((1, 128), jnp.int32),
            pltpu.VMEM((count, 128, 128), BF16),
            pltpu.SemaphoreType.DMA((PIECES + 2,)),
        ],
        name="pack",
    )(channel_loc.reshape(1, 128), channel_valid.reshape(1, 128), blocks)


def split3(x):
    hi = x.astype(BF16)
    rest = x - hi.astype(F32)
    mid = rest.astype(BF16)
    low = (rest - mid.astype(F32)).astype(BF16)
    return hi, mid, low


def skew_sum(x):
    total = x[0:8]
    for g in range(1, 16):
        total = total + pltpu.roll(x[8 * g : 8 * g + 8], 128 - 8 * g, 1)
    out = total[0:1]
    for s in range(1, 8):
        out = out + pltpu.roll(total[s : s + 1], 128 - s, 1)
    return out


def exact_dot(x, picks):
    hi, mid, rest = split3(x)
    return dot_nn(hi, picks) + dot_nn(mid, picks) + dot_nn(rest, picks)


CHUNK = 32
NCHUNK = 128 // CHUNK


def main_kernel(owner_hbm, y_ref, o_ref, owner_row_ref, sem, x_s, w_s, lin_s, mask_s, lin_acc, acc_s, pw_s):
    copy = pltpu.make_async_copy(owner_hbm, owner_row_ref, sem)
    copy.start()
    lane = iota((128, 128), 1)
    row = iota((128, 128), 0)
    sign = jnp.where(row // 32 % 2 == 1, 1.0, -1.0)
    swap = jnp.where(row == jnp.where(lane // 32 % 2 == 0, lane + 32, lane - 32), sign, 0.0).astype(BF16)
    bits_t = y_ref[:, 128:136, :].astype(F32).reshape(128, 128)
    bits = jnp.transpose(bits_t)
    own = [jnp.where(lane // 64 == f, 1.0, 0.0).astype(BF16) for f in range(2)]

    edge = jnp.where(row > lane, 1.0, jnp.where(row < lane, 0.0, -1.0))
    suffix = jnp.zeros((128, 128), F32)
    for r in reversed(range(16)):
        late = jnp.broadcast_to(bits_t[:, r : r + 1], (128, 128))
        gap = late - jnp.broadcast_to(bits[r : r + 1, :], (128, 128))
        mask_s[r] = jnp.minimum(jnp.maximum(edge + gap, 0.0), 1.0)
        x = y_ref[:, 8 * r : 8 * r + 8, :].astype(F32).reshape(128, 128)
        xb = x.astype(BF16)
        w_s[r, 0:128, :] = xb
        w_s[r, 128:256, :] = dot_nn(xb, swap).astype(BF16)
        hi = suffix.astype(BF16)
        low = (suffix - hi.astype(F32)).astype(BF16)
        for f in range(2):
            mine = xb * own[f]
            for c in range(NCHUNK):
                x_s[f, c, CHUNK * r : CHUNK * r + CHUNK, :] = mine[CHUNK * c : CHUNK * c + CHUNK]
            lin_s[f, :, 256 * r : 256 * r + 128] = hi * own[f]
            lin_s[f, :, 256 * r + 128 : 256 * r + 256] = low * own[f]
        suffix = suffix + x

    acc_s[...] = jnp.zeros(acc_s.shape, F32)

    keep_diag = row >= lane

    def one_freq(f):
        lin = jnp.zeros((128, 256), F32)
        lin_acc[f] = jnp.zeros((128, 256), F32)
        for r in range(16):
            w = w_s[r]
            lin = lin + dot_nt(lin_s[f, :, 256 * r : 256 * r + 256], jnp.concatenate([w, w], 1))
            for c in range(NCHUNK):
                rows = slice(CHUNK * c, CHUNK * c + CHUNK)
                prod = dot_nt(x_s[f, c, CHUNK * r :, :], w)
                mask = mask_s[r, rows]
                for u in range(r, 16):
                    at = CHUNK * (u - r)
                    re = prod[at : at + CHUNK, 0:128]
                    im = prod[at : at + CHUNK, 128:256]
                    gain = lax.rsqrt(jnp.maximum(re * re + im * im, 1.0))
                    if u == r:
                        lin_acc[f, rows, 0:128] += re * mask
                        lin_acc[f, rows, 128:256] += im * mask
                        gain = gain * mask
                        acc_re = re * gain
                        acc_im = im * gain
                    else:
                        acc_re = acc_re + re * gain
                        acc_im = acc_im + im * gain
                acc_s[f, rows, 0:128] += acc_re
                acc_s[f, rows, 128:256] += acc_im
        for part in range(4):
            cols = slice(128 * (part % 2), 128 * (part % 2) + 128)
            full = lin[:, cols] + lin_acc[f, :, cols] if part < 2 else acc_s[f, :, cols]
            low = skew_sum(jnp.where(keep_diag, full, 0.0))
            up = skew_sum(jnp.where(keep_diag, 0.0, full))
            pw_s[f, part : part + 1, 0:128] = low
            pw_s[f, part : part + 1, 128:256] = up if part % 2 == 0 else -up

    pw_s[...] = jnp.zeros(pw_s.shape, F32)
    for f in range(2):
        one_freq(f)

    low_pick = jnp.where((lane + row) % 128 == 0, 1.0, 0.0)
    up_pick = jnp.where(row == lane + 1, 1.0, 0.0)
    unpick = jnp.concatenate([low_pick, up_pick], 0).astype(BF16)
    sums = exact_dot(pw_s[...].reshape(16, 256), unpick)
    out = []
    for f in range(2):
        part = [sums[8 * f + p : 8 * f + p + 1] for p in range(4)]
        power = part[2] * part[2] + part[3] * part[3]
        out += [part[0], part[1], part[0] * power, part[1] * power]
    copy.wait()
    owner_row = jnp.broadcast_to(owner_row_ref[...], (128, 128))
    earlier = (owner_row == jnp.transpose(owner_row)) & (row < lane)
    rank = jnp.sum(jnp.where(earlier, 1.0, 0.0), 0, keepdims=True).astype(jnp.int32)
    slot = 16 * owner_row_ref[...] + rank
    place = jnp.where(iota((256, 128), 0) == slot, 1.0, 0.0).astype(BF16)
    by_bin = jnp.transpose(jnp.concatenate(out + [jnp.zeros((120, 128), F32)], 0))
    hi, mid, rest = split3(by_bin)
    placed = dot_nn(place, hi) + dot_nn(place, mid) + dot_nn(place, rest)
    o_ref[...] = placed[:, 0:8]


def bin_sums(bin_owner, received):
    vmem = pl.BlockSpec(memory_space=pltpu.VMEM)
    return pl.pallas_call(
        main_kernel,
        in_specs=[pl.BlockSpec(memory_space=pl.ANY), vmem],
        out_specs=vmem,
        out_shape=pltpu.VMEM((256, 8), F32),
        scratch_shapes=[
            pltpu.VMEM((1, 128), jnp.int32),
            pltpu.SemaphoreType.DMA(()),
            pltpu.VMEM((2, NCHUNK, 16 * CHUNK, 128), BF16),
            pltpu.VMEM((16, 256, 128), BF16),
            pltpu.VMEM((2, 128, 16 * 256), BF16),
            pltpu.VMEM((16, 128, 128), F32),
            pltpu.VMEM((2, 128, 256), F32),
            pltpu.VMEM((2, 128, 256), F32),
            pltpu.VMEM((2, 8, 256), F32),
        ],
        name="bin_sums",
    )(bin_owner.reshape(1, 128), received)


def lag_tables():
    lane = np.arange(128)
    f0 = lane // 8 * 2 + lane % 8 // 4
    imag = lane % 2
    weight = np.full((16, 128), 2.0) * np.where(f0 % 2, -1.0, 1.0)
    weight[0, f0 == 0] = 1.0
    turn0 = 2 * np.pi * (np.arange(32)[:, None] * np.arange(16) % 32) / 32
    first = np.concatenate([np.cos(turn0), np.sin(turn0)], 0)
    turn1 = 2 * np.pi * (np.arange(128)[:, None] * f0 % 1024) / 1024
    t1 = np.where(imag, -np.sin(turn1), np.cos(turn1))
    t2 = np.where(imag, -np.cos(turn1), -np.sin(turn1))
    turn2 = 2 * np.pi * (np.arange(8)[:, None] * f0 % 8) / 8
    which = [lane % 4 // 2 == 0, lane % 4 // 2 == 1]
    last = [np.concatenate([np.cos(turn2) * w, -np.sin(turn2) * w], 1) for w in which]
    return [np.asarray(t, np.float32) for t in (weight, first, np.stack([t1, t2]), np.concatenate(last, 0))]


def finish_kernel(x_ref, weight_ref, first_ref, twiddle_ref, last_ref, lin_ref, phase_ref):
    spread = jnp.where(iota((8, 128), 0) == iota((8, 128), 1) % 8, 1.0, 0.0).astype(BF16)
    wide = exact_dot(x_ref[...], spread)
    wide = jnp.where(iota((256, 128), 0) % 16 == iota((256, 128), 1) // 8, wide, 0.0)
    z = jnp.sum(wide.reshape(16, 16, 128), 1) * weight_ref[...]
    high = lax.Precision.HIGHEST
    v = jnp.dot(first_ref[...], z, precision=high, preferred_element_type=F32)
    g = jnp.concatenate([v[0:32]] * 4, 0)
    h = jnp.concatenate([v[32:64]] * 4, 0)
    t1 = twiddle_ref[0]
    t2 = twiddle_ref[1]
    q = jnp.concatenate([g * t1 + h * t2, h * t1 - g * t2], 1)
    series = lax.dot_general(
        last_ref[...], q, (((1,), (1,)), ((), ())), precision=high, preferred_element_type=F32
    )
    for i, o_ref in enumerate((lin_ref, phase_ref)):
        c = series[8 * i : 8 * i + 8]
        o_ref[...] = c / jnp.sqrt(jnp.sum(c * c) * (1.0 / 1024) + 1e-06)


def finish(mine):
    vmem = pl.BlockSpec(memory_space=pltpu.VMEM)
    return pl.pallas_call(
        finish_kernel,
        in_specs=[vmem] * 5,
        out_specs=[vmem] * 2,
        out_shape=[jax.ShapeDtypeStruct((8, 128), F32)] * 2,
        name="finish",
    )(mine, *[in_vmem(jnp.asarray(t)) for t in lag_tables()])


def in_vmem(x):
    return pltpu.with_memory_space_constraint(x, pltpu.VMEM)


def exchange(x, axis):
    return lax.all_to_all(x, axis, split_axis=0, concat_axis=0, tiled=True)


def on_device(spectra, channel_loc, channel_valid, bin_owner):
    blocks = spectra.reshape(lax.axis_size("loop"), 128, 128)
    received = exchange(pack(channel_loc, channel_valid, blocks), "loop")
    received = in_vmem(received)
    sums = bin_sums(bin_owner, received)
    linear, phase = finish(in_vmem(exchange(sums, ("stack", "loop"))))
    return linear.reshape(1, 1, -1), phase.reshape(1, 1, -1)


def solution(mesh):
    in_specs = (P("stack", None, None, "loop"), P("loop"), P("loop"), P())
    out_specs = (P("stack", "loop", None), P("stack", "loop", None))
    return jax.shard_map(
        on_device, mesh=mesh, in_specs=in_specs, out_specs=out_specs, check_vma=False
    )
```

```python
import jax
import jax.numpy as jnp
import numpy as np
from jax import lax
from jax.experimental import pallas as pl
from jax.experimental.pallas import tpu as pltpu
from jax.sharding import PartitionSpec as P

F32 = jnp.float32
BF16 = jnp.bfloat16


def iota(shape, dim):
    return lax.broadcasted_iota(jnp.int32, shape, dim)


def dot_nt(a, b):
    return lax.dot_general(a, b, (((1,), (1,)), ((), ())), preferred_element_type=F32)


def dot_nn(a, b):
    return lax.dot_general(a, b, (((1,), (0,)), ((), ())), preferred_element_type=F32)


PIECES = 1


def pack_kernel(loc_hbm, valid_hbm, x_hbm, o_ref, loc_ref, valid_ref, x_ref, sems):
    count = x_ref.shape[0]
    size = count // PIECES
    copies = [
        pltpu.make_async_copy(x_hbm.at[pl.ds(i * size, size)], x_ref.at[pl.ds(i * size, size)], sems.at[i])
        for i in range(PIECES)
    ]
    small = [
        pltpu.make_async_copy(loc_hbm, loc_ref, sems.at[PIECES]),
        pltpu.make_async_copy(valid_hbm, valid_ref, sems.at[PIECES + 1]),
    ]
    for copy in small + copies:
        copy.start()
    for copy in small:
        copy.wait()
    row = iota((128, 128), 0)
    col = iota((128, 128), 1)
    valid = jnp.broadcast_to(valid_ref[...].astype(F32), (128, 128))
    pick = jnp.where(col == 16 * (row % 8) + row // 8, valid, 0.0).astype(BF16)
    jit = jnp.broadcast_to((loc_ref[...] & 1).astype(F32), (16, 128))
    jit = jnp.where(iota((16, 128), 1) // 16 == iota((16, 128), 0), jit, 0.0).astype(BF16)
    spread = jnp.where(col == row % 16, 1.0, 0.0).astype(BF16)
    bits = dot_nn(jit, spread)[0:8].astype(BF16)
    for i, copy in enumerate(copies):
        copy.wait()
        for g in range(i * size, (i + 1) * size):
            o_ref[g, 0:128] = dot_nt(pick, x_ref[g]).astype(BF16)
            o_ref[g, 128:136] = bits


def pack(channel_loc, channel_valid, blocks):
    count = blocks.shape[0]
    return pl.pallas_call(
        pack_kernel,
        in_specs=[pl.BlockSpec(memory_space=pl.ANY)] * 3,
        out_specs=pl.BlockSpec(memory_space=pltpu.VMEM),
        out_shape=pltpu.VMEM((count, 136, 128), BF16),
        scratch_shapes=[
            pltpu.VMEM((1, 128), jnp.int32),
            pltpu.VMEM((1, 128), jnp.int32),
            pltpu.VMEM((count, 128, 128), BF16),
            pltpu.SemaphoreType.DMA((PIECES + 2,)),
        ],
        name="pack",
    )(channel_loc.reshape(1, 128), channel_valid.reshape(1, 128), blocks)


def split3(x):
    hi = x.astype(BF16)
    rest = x - hi.astype(F32)
    mid = rest.astype(BF16)
    low = (rest - mid.astype(F32)).astype(BF16)
    return hi, mid, low


def skew_sum(x):
    total = x[0:8]
    for g in range(1, 16):
        total = total + pltpu.roll(x[8 * g : 8 * g + 8], 128 - 8 * g, 1)
    out = total[0:1]
    for s in range(1, 8):
        out = out + pltpu.roll(total[s : s + 1], 128 - s, 1)
    return out


def exact_dot(x, picks):
    hi, mid, rest = split3(x)
    return dot_nn(hi, picks) + dot_nn(mid, picks) + dot_nn(rest, picks)


CHUNK = 32
NCHUNK = 128 // CHUNK


def main_kernel(owner_hbm, y_ref, o_ref, owner_row_ref, sem, x_s, w_s, lin_s, mask_s, lin_acc, acc_s, pw_s):
    copy = pltpu.make_async_copy(owner_hbm, owner_row_ref, sem)
    copy.start()
    lane = iota((128, 128), 1)
    row = iota((128, 128), 0)
    sign = jnp.where(row // 32 % 2 == 1, 1.0, -1.0)
    swap = jnp.where(row == jnp.where(lane // 32 % 2 == 0, lane + 32, lane - 32), sign, 0.0).astype(BF16)
    bits_t = y_ref[:, 128:136, :].astype(F32).reshape(128, 128)
    bits = jnp.transpose(bits_t)
    own = [jnp.where(lane // 64 == f, 1.0, 0.0).astype(BF16) for f in range(2)]

    edge = jnp.where(row > lane, 1.0, jnp.where(row < lane, 0.0, -1.0))
    suffix = jnp.zeros((128, 128), F32)
    for r in reversed(range(16)):
        late = jnp.broadcast_to(bits_t[:, r : r + 1], (128, 128))
        gap = late - jnp.broadcast_to(bits[r : r + 1, :], (128, 128))
        mask_s[r] = jnp.minimum(jnp.maximum(edge + gap, 0.0), 1.0)
        x = y_ref[:, 8 * r : 8 * r + 8, :].astype(F32).reshape(128, 128)
        xb = x.astype(BF16)
        w_s[r, 0:128, :] = xb
        w_s[r, 128:256, :] = dot_nn(xb, swap).astype(BF16)
        hi = suffix.astype(BF16)
        low = (suffix - hi.astype(F32)).astype(BF16)
        for f in range(2):
            mine = xb * own[f]
            for c in range(NCHUNK):
                x_s[f, c, CHUNK * r : CHUNK * r + CHUNK, :] = mine[CHUNK * c : CHUNK * c + CHUNK]
            lin_s[f, :, 256 * r : 256 * r + 128] = hi * own[f]
            lin_s[f, :, 256 * r + 128 : 256 * r + 256] = low * own[f]
        suffix = suffix + x

    acc_s[...] = jnp.zeros(acc_s.shape, F32)

    keep_diag = row >= lane

    def one_freq(f):
        lin = jnp.zeros((128, 256), F32)
        lin_acc[f] = jnp.zeros((128, 256), F32)
        for r in range(16):
            w = w_s[r]
            lin = lin + dot_nt(lin_s[f, :, 256 * r : 256 * r + 256], jnp.concatenate([w, w], 1))
            for c in range(NCHUNK):
                rows = slice(CHUNK * c, CHUNK * c + CHUNK)
                prod = dot_nt(x_s[f, c, CHUNK * r :, :], w)
                mask = mask_s[r, rows]
                for u in range(r, 16):
                    at = CHUNK * (u - r)
                    re = prod[at : at + CHUNK, 0:128]
                    im = prod[at : at + CHUNK, 128:256]
                    gain = lax.rsqrt(jnp.maximum(re * re + im * im, 1.0))
                    if u == r:
                        lin_acc[f, rows, 0:128] += re * mask
                        lin_acc[f, rows, 128:256] += im * mask
                        gain = gain * mask
                        acc_re = re * gain
                        acc_im = im * gain
                    else:
                        acc_re = acc_re + re * gain
                        acc_im = acc_im + im * gain
                acc_s[f, rows, 0:128] += acc_re
                acc_s[f, rows, 128:256] += acc_im
        for part in range(4):
            cols = slice(128 * (part % 2), 128 * (part % 2) + 128)
            full = lin[:, cols] + lin_acc[f, :, cols] if part < 2 else acc_s[f, :, cols]
            low = skew_sum(jnp.where(keep_diag, full, 0.0))
            up = skew_sum(jnp.where(keep_diag, 0.0, full))
            pw_s[f, part : part + 1, 0:128] = low
            pw_s[f, part : part + 1, 128:256] = up if part % 2 == 0 else -up

    pw_s[...] = jnp.zeros(pw_s.shape, F32)
    for f in range(2):
        one_freq(f)

    low_pick = jnp.where((lane + row) % 128 == 0, 1.0, 0.0)
    up_pick = jnp.where(row == lane + 1, 1.0, 0.0)
    unpick = jnp.concatenate([low_pick, up_pick], 0).astype(BF16)
    sums = exact_dot(pw_s[...].reshape(16, 256), unpick)
    out = []
    for f in range(2):
        part = [sums[8 * f + p : 8 * f + p + 1] for p in range(4)]
        power = part[2] * part[2] + part[3] * part[3]
        out += [part[0], part[1], part[0] * power, part[1] * power]
    copy.wait()
    owner_row = jnp.broadcast_to(owner_row_ref[...], (128, 128))
    earlier = (owner_row == jnp.transpose(owner_row)) & (row < lane)
    rank = jnp.sum(jnp.where(earlier, 1.0, 0.0), 0, keepdims=True).astype(jnp.int32)
    slot = 16 * owner_row_ref[...] + rank
    place = jnp.where(iota((256, 128), 0) == slot, 1.0, 0.0).astype(BF16)
    by_bin = jnp.transpose(jnp.concatenate(out + [jnp.zeros((120, 128), F32)], 0))
    hi, mid, rest = split3(by_bin)
    placed = dot_nn(place, hi) + dot_nn(place, mid) + dot_nn(place, rest)
    o_ref[...] = placed[:, 0:8]


def bin_sums(bin_owner, received):
    vmem = pl.BlockSpec(memory_space=pltpu.VMEM)
    return pl.pallas_call(
        main_kernel,
        in_specs=[pl.BlockSpec(memory_space=pl.ANY), vmem],
        out_specs=vmem,
        out_shape=pltpu.VMEM((256, 8), F32),
        scratch_shapes=[
            pltpu.VMEM((1, 128), jnp.int32),
            pltpu.SemaphoreType.DMA(()),
            pltpu.VMEM((2, NCHUNK, 16 * CHUNK, 128), BF16),
            pltpu.VMEM((16, 256, 128), BF16),
            pltpu.VMEM((2, 128, 16 * 256), BF16),
            pltpu.VMEM((16, 128, 128), F32),
            pltpu.VMEM((2, 128, 256), F32),
            pltpu.VMEM((2, 128, 256), F32),
            pltpu.VMEM((2, 8, 256), F32),
        ],
        name="bin_sums",
    )(bin_owner.reshape(1, 128), received)


def lag_tables():
    lane = np.arange(128)
    f0 = lane // 8 * 2 + lane % 8 // 4
    imag = lane % 2
    weight = np.full((16, 128), 2.0) * np.where(f0 % 2, -1.0, 1.0)
    weight[0, f0 == 0] = 1.0
    turn0 = 2 * np.pi * (np.arange(32)[:, None] * np.arange(16) % 32) / 32
    first = np.concatenate([np.cos(turn0), np.sin(turn0)], 0)
    turn1 = 2 * np.pi * (np.arange(128)[:, None] * f0 % 1024) / 1024
    t1 = np.where(imag, -np.sin(turn1), np.cos(turn1))
    t2 = np.where(imag, -np.cos(turn1), -np.sin(turn1))
    turn2 = 2 * np.pi * (np.arange(8)[:, None] * f0 % 8) / 8
    which = [lane % 4 // 2 == 0, lane % 4 // 2 == 1]
    last = [np.concatenate([np.cos(turn2) * w, -np.sin(turn2) * w], 1) for w in which]
    return [np.asarray(t, np.float32) for t in (weight, first, np.stack([t1, t2]), np.concatenate(last, 0))]


def dot3(a, b, dim):
    ah = a.astype(BF16)
    al = (a - ah.astype(F32)).astype(BF16)
    bh = b.astype(BF16)
    bl = (b - bh.astype(F32)).astype(BF16)
    dot = dot_nt if dim else dot_nn
    return dot(ah, bh) + (dot(ah, bl) + dot(al, bh))


def finish_kernel(x_ref, weight_ref, first_ref, twiddle_ref, last_ref, lin_ref, phase_ref):
    spread = jnp.where(iota((8, 128), 0) == iota((8, 128), 1) % 8, 1.0, 0.0).astype(BF16)
    wide = exact_dot(x_ref[...], spread)
    wide = jnp.where(iota((256, 128), 0) % 16 == iota((256, 128), 1) // 8, wide, 0.0)
    z = jnp.sum(wide.reshape(16, 16, 128), 1) * weight_ref[...]
    v = dot3(first_ref[...], z, 0)
    g = jnp.concatenate([v[0:32]] * 4, 0)
    h = jnp.concatenate([v[32:64]] * 4, 0)
    t1 = twiddle_ref[0]
    t2 = twiddle_ref[1]
    q = jnp.concatenate([g * t1 + h * t2, h * t1 - g * t2], 1)
    series = dot3(last_ref[...], q, 1)
    for i, o_ref in enumerate((lin_ref, phase_ref)):
        c = series[8 * i : 8 * i + 8]
        o_ref[...] = c / jnp.sqrt(jnp.sum(c * c) * (1.0 / 1024) + 1e-06)


def finish(mine):
    vmem = pl.BlockSpec(memory_space=pltpu.VMEM)
    return pl.pallas_call(
        finish_kernel,
        in_specs=[vmem] * 5,
        out_specs=[vmem] * 2,
        out_shape=[jax.ShapeDtypeStruct((8, 128), F32)] * 2,
        name="finish",
    )(mine, *[in_vmem(jnp.asarray(t)) for t in lag_tables()])


def in_vmem(x):
    return pltpu.with_memory_space_constraint(x, pltpu.VMEM)


def exchange(x, axis):
    return lax.all_to_all(x, axis, split_axis=0, concat_axis=0, tiled=True)


def on_device(spectra, channel_loc, channel_valid, bin_owner):
    blocks = spectra.reshape(lax.axis_size("loop"), 128, 128)
    received = exchange(pack(channel_loc, channel_valid, blocks), "loop")
    received = in_vmem(received)
    sums = bin_sums(bin_owner, received)
    linear, phase = finish(in_vmem(exchange(sums, ("stack", "loop"))))
    return linear.reshape(1, 1, -1), phase.reshape(1, 1, -1)


def solution(mesh):
    in_specs = (P("stack", None, None, "loop"), P("loop"), P("loop"), P())
    out_specs = (P("stack", "loop", None), P("stack", "loop", None))
    return jax.shard_map(
        on_device, mesh=mesh, in_specs=in_specs, out_specs=out_specs, check_vma=False
    )
```

```python
import jax
import jax.numpy as jnp
import numpy as np
from jax import lax
from jax.experimental import pallas as pl
from jax.experimental.pallas import tpu as pltpu
from jax.sharding import PartitionSpec as P

F32 = jnp.float32
BF16 = jnp.bfloat16


def iota(shape, dim):
    return lax.broadcasted_iota(jnp.int32, shape, dim)


def dot_nt(a, b):
    return lax.dot_general(a, b, (((1,), (1,)), ((), ())), preferred_element_type=F32)


def dot_nn(a, b):
    return lax.dot_general(a, b, (((1,), (0,)), ((), ())), preferred_element_type=F32)


PIECES = 1


def pack_kernel(loc_hbm, valid_hbm, x_hbm, o_ref, loc_ref, valid_ref, x_ref, sems):
    count = x_ref.shape[0]
    size = count // PIECES
    copies = [
        pltpu.make_async_copy(x_hbm.at[pl.ds(i * size, size)], x_ref.at[pl.ds(i * size, size)], sems.at[i])
        for i in range(PIECES)
    ]
    small = [
        pltpu.make_async_copy(loc_hbm, loc_ref, sems.at[PIECES]),
        pltpu.make_async_copy(valid_hbm, valid_ref, sems.at[PIECES + 1]),
    ]
    for copy in small + copies:
        copy.start()
    for copy in small:
        copy.wait()
    row = iota((128, 128), 0)
    col = iota((128, 128), 1)
    valid = jnp.broadcast_to(valid_ref[...].astype(F32), (128, 128))
    pick = jnp.where(col == 16 * (row % 8) + row // 8, valid, 0.0).astype(BF16)
    jit = jnp.broadcast_to((loc_ref[...] & 1).astype(F32), (16, 128))
    jit = jnp.where(iota((16, 128), 1) // 16 == iota((16, 128), 0), jit, 0.0).astype(BF16)
    spread = jnp.where(col == row % 16, 1.0, 0.0).astype(BF16)
    bits = dot_nn(jit, spread)[0:8].astype(BF16)
    for i, copy in enumerate(copies):
        copy.wait()
        for g in range(i * size, (i + 1) * size):
            o_ref[g, 0:128] = dot_nt(pick, x_ref[g]).astype(BF16)
            o_ref[g, 128:136] = bits


def pack(channel_loc, channel_valid, blocks):
    count = blocks.shape[0]
    return pl.pallas_call(
        pack_kernel,
        in_specs=[pl.BlockSpec(memory_space=pl.ANY)] * 3,
        out_specs=pl.BlockSpec(memory_space=pltpu.VMEM),
        out_shape=pltpu.VMEM((count, 136, 128), BF16),
        scratch_shapes=[
            pltpu.VMEM((1, 128), jnp.int32),
            pltpu.VMEM((1, 128), jnp.int32),
            pltpu.VMEM((count, 128, 128), BF16),
            pltpu.SemaphoreType.DMA((PIECES + 2,)),
        ],
        name="pack",
    )(channel_loc.reshape(1, 128), channel_valid.reshape(1, 128), blocks)


def split3(x):
    hi = x.astype(BF16)
    rest = x - hi.astype(F32)
    mid = rest.astype(BF16)
    low = (rest - mid.astype(F32)).astype(BF16)
    return hi, mid, low


def skew_sum(x):
    total = x[0:8]
    for g in range(1, 16):
        total = total + pltpu.roll(x[8 * g : 8 * g + 8], 128 - 8 * g, 1)
    out = total[0:1]
    for s in range(1, 8):
        out = out + pltpu.roll(total[s : s + 1], 128 - s, 1)
    return out


def exact_dot(x, picks):
    hi, mid, rest = split3(x)
    return dot_nn(hi, picks) + dot_nn(mid, picks) + dot_nn(rest, picks)


CHUNK = 32
NCHUNK = 128 // CHUNK


def main_kernel(owner_hbm, y_ref, o_ref, owner_row_ref, sem, x_s, w_s, lin_s, mask_s, lin_acc, acc_s, pw_s):
    copy = pltpu.make_async_copy(owner_hbm, owner_row_ref, sem)
    copy.start()
    lane = iota((128, 128), 1)
    row = iota((128, 128), 0)
    sign = jnp.where(row // 32 % 2 == 1, 1.0, -1.0)
    swap = jnp.where(row == jnp.where(lane // 32 % 2 == 0, lane + 32, lane - 32), sign, 0.0).astype(BF16)
    bits_t = y_ref[:, 128:136, :].astype(F32).reshape(128, 128)
    bits = jnp.transpose(bits_t)
    own = [jnp.where(lane // 64 == f, 1.0, 0.0).astype(BF16) for f in range(2)]

    edge = jnp.where(row > lane, 1.0, jnp.where(row < lane, 0.0, -1.0))
    suffix = jnp.zeros((128, 128), F32)
    for r in reversed(range(16)):
        late = jnp.broadcast_to(bits_t[:, r : r + 1], (128, 128))
        gap = late - jnp.broadcast_to(bits[r : r + 1, :], (128, 128))
        mask_s[r] = jnp.minimum(jnp.maximum(edge + gap, 0.0), 1.0)
        x = y_ref[:, 8 * r : 8 * r + 8, :].astype(F32).reshape(128, 128)
        xb = x.astype(BF16)
        w_s[r, 0:128, :] = xb
        w_s[r, 128:256, :] = dot_nn(xb, swap).astype(BF16)
        hi = suffix.astype(BF16)
        low = (suffix - hi.astype(F32)).astype(BF16)
        for f in range(2):
            mine = xb * own[f]
            for c in range(NCHUNK):
                x_s[f, c, CHUNK * r : CHUNK * r + CHUNK, :] = mine[CHUNK * c : CHUNK * c + CHUNK]
            lin_s[f, r, 0] = hi * own[f]
            lin_s[f, r, 1] = low * own[f]
        suffix = suffix + x

    acc_s[...] = jnp.zeros(acc_s.shape, F32)

    keep_diag = row >= lane

    def one_freq(f):
        lin = jnp.zeros((128, 256), F32)
        lin_acc[f] = jnp.zeros((128, 256), F32)
        for r in range(16):
            w = w_s[r]
            lin = lin + dot_nt(jnp.concatenate([lin_s[f, r, 0], lin_s[f, r, 1]], 1), jnp.concatenate([w, w], 1))
            for c in range(NCHUNK):
                rows = slice(CHUNK * c, CHUNK * c + CHUNK)
                prod = dot_nt(x_s[f, c, CHUNK * r :, :], w)
                mask = mask_s[r, rows]
                for u in range(r, 16):
                    at = CHUNK * (u - r)
                    re = prod[at : at + CHUNK, 0:128]
                    im = prod[at : at + CHUNK, 128:256]
                    gain = lax.rsqrt(jnp.maximum(re * re + im * im, 1.0))
                    if u == r:
                        lin_acc[f, rows, 0:128] += re * mask
                        lin_acc[f, rows, 128:256] += im * mask
                        gain = gain * mask
                        acc_re = re * gain
                        acc_im = im * gain
                    else:
                        acc_re = acc_re + re * gain
                        acc_im = acc_im + im * gain
                acc_s[f, rows, 0:128] += acc_re
                acc_s[f, rows, 128:256] += acc_im
        for part in range(4):
            cols = slice(128 * (part % 2), 128 * (part % 2) + 128)
            full = lin[:, cols] + lin_acc[f, :, cols] if part < 2 else acc_s[f, :, cols]
            low = skew_sum(jnp.where(keep_diag, full, 0.0))
            up = skew_sum(jnp.where(keep_diag, 0.0, full))
            pw_s[f, part : part + 1, 0:128] = low
            pw_s[f, part : part + 1, 128:256] = up if part % 2 == 0 else -up

    pw_s[...] = jnp.zeros(pw_s.shape, F32)
    for f in range(2):
        one_freq(f)

    low_pick = jnp.where((lane + row) % 128 == 0, 1.0, 0.0)
    up_pick = jnp.where(row == lane + 1, 1.0, 0.0)
    unpick = jnp.concatenate([low_pick, up_pick], 0).astype(BF16)
    sums = exact_dot(pw_s[...].reshape(16, 256), unpick)
    out = []
    for f in range(2):
        part = [sums[8 * f + p : 8 * f + p + 1] for p in range(4)]
        power = part[2] * part[2] + part[3] * part[3]
        out += [part[0], part[1], part[0] * power, part[1] * power]
    copy.wait()
    owner_row = jnp.broadcast_to(owner_row_ref[...], (128, 128))
    earlier = (owner_row == jnp.transpose(owner_row)) & (row < lane)
    rank = jnp.sum(jnp.where(earlier, 1.0, 0.0), 0, keepdims=True).astype(jnp.int32)
    slot = 16 * owner_row_ref[...] + rank
    place = jnp.where(iota((256, 128), 0) == slot, 1.0, 0.0).astype(BF16)
    by_bin = jnp.transpose(jnp.concatenate(out + [jnp.zeros((120, 128), F32)], 0))
    hi, mid, rest = split3(by_bin)
    placed = dot_nn(place, hi) + dot_nn(place, mid) + dot_nn(place, rest)
    o_ref[...] = placed[:, 0:8]


def bin_sums(bin_owner, received):
    vmem = pl.BlockSpec(memory_space=pltpu.VMEM)
    return pl.pallas_call(
        main_kernel,
        in_specs=[pl.BlockSpec(memory_space=pl.ANY), vmem],
        out_specs=vmem,
        out_shape=pltpu.VMEM((256, 8), F32),
        scratch_shapes=[
            pltpu.VMEM((1, 128), jnp.int32),
            pltpu.SemaphoreType.DMA(()),
            pltpu.VMEM((2, NCHUNK, 16 * CHUNK, 128), BF16),
            pltpu.VMEM((16, 256, 128), BF16),
            pltpu.VMEM((2, 16, 2, 128, 128), BF16),
            pltpu.VMEM((16, 128, 128), F32),
            pltpu.VMEM((2, 128, 256), F32),
            pltpu.VMEM((2, 128, 256), F32),
            pltpu.VMEM((2, 8, 256), F32),
        ],
        name="bin_sums",
    )(bin_owner.reshape(1, 128), received)


def lag_tables():
    lane = np.arange(128)
    f0 = lane // 8 * 2 + lane % 8 // 4
    imag = lane % 2
    weight = np.full((16, 128), 2.0) * np.where(f0 % 2, -1.0, 1.0)
    weight[0, f0 == 0] = 1.0
    turn0 = 2 * np.pi * (np.arange(32)[:, None] * np.arange(16) % 32) / 32
    first = np.concatenate([np.cos(turn0), np.sin(turn0)], 0)
    turn1 = 2 * np.pi * (np.arange(128)[:, None] * f0 % 1024) / 1024
    t1 = np.where(imag, -np.sin(turn1), np.cos(turn1))
    t2 = np.where(imag, -np.cos(turn1), -np.sin(turn1))
    turn2 = 2 * np.pi * (np.arange(8)[:, None] * f0 % 8) / 8
    which = [lane % 4 // 2 == 0, lane % 4 // 2 == 1]
    last = [np.concatenate([np.cos(turn2) * w, -np.sin(turn2) * w], 1) for w in which]
    return [np.asarray(t, np.float32) for t in (weight, first, np.stack([t1, t2]), np.concatenate(last, 0))]


def dot3(a, b, dim):
    ah = a.astype(BF16)
    al = (a - ah.astype(F32)).astype(BF16)
    bh = b.astype(BF16)
    bl = (b - bh.astype(F32)).astype(BF16)
    dot = dot_nt if dim else dot_nn
    return dot(ah, bh) + (dot(ah, bl) + dot(al, bh))


def finish_kernel(x_ref, weight_ref, first_ref, twiddle_ref, last_ref, lin_ref, phase_ref):
    spread = jnp.where(iota((8, 128), 0) == iota((8, 128), 1) % 8, 1.0, 0.0).astype(BF16)
    wide = exact_dot(x_ref[...], spread)
    wide = jnp.where(iota((256, 128), 0) % 16 == iota((256, 128), 1) // 8, wide, 0.0)
    z = jnp.sum(wide.reshape(16, 16, 128), 1) * weight_ref[...]
    v = dot3(first_ref[...], z, 0)
    g = jnp.concatenate([v[0:32]] * 4, 0)
    h = jnp.concatenate([v[32:64]] * 4, 0)
    t1 = twiddle_ref[0]
    t2 = twiddle_ref[1]
    q = jnp.concatenate([g * t1 + h * t2, h * t1 - g * t2], 1)
    series = dot3(last_ref[...], q, 1)
    for i, o_ref in enumerate((lin_ref, phase_ref)):
        c = series[8 * i : 8 * i + 8]
        o_ref[...] = c / jnp.sqrt(jnp.sum(c * c) * (1.0 / 1024) + 1e-06)


def finish(mine):
    vmem = pl.BlockSpec(memory_space=pltpu.VMEM)
    return pl.pallas_call(
        finish_kernel,
        in_specs=[vmem] * 5,
        out_specs=[vmem] * 2,
        out_shape=[jax.ShapeDtypeStruct((8, 128), F32)] * 2,
        name="finish",
    )(mine, *[in_vmem(jnp.asarray(t)) for t in lag_tables()])


def in_vmem(x):
    return pltpu.with_memory_space_constraint(x, pltpu.VMEM)


def exchange(x, axis):
    return lax.all_to_all(x, axis, split_axis=0, concat_axis=0, tiled=True)


def on_device(spectra, channel_loc, channel_valid, bin_owner):
    blocks = spectra.reshape(lax.axis_size("loop"), 128, 128)
    received = exchange(pack(channel_loc, channel_valid, blocks), "loop")
    received = in_vmem(received)
    sums = bin_sums(bin_owner, received)
    linear, phase = finish(in_vmem(exchange(sums, ("stack", "loop"))))
    return linear.reshape(1, 1, -1), phase.reshape(1, 1, -1)


def solution(mesh):
    in_specs = (P("stack", None, None, "loop"), P("loop"), P("loop"), P())
    out_specs = (P("stack", "loop", None), P("stack", "loop", None))
    return jax.shard_map(
        on_device, mesh=mesh, in_specs=in_specs, out_specs=out_specs, check_vma=False
    )
```

```python
import jax
import jax.numpy as jnp
import numpy as np
from jax import lax
from jax.experimental import pallas as pl
from jax.experimental.pallas import tpu as pltpu
from jax.sharding import PartitionSpec as P

F32 = jnp.float32
BF16 = jnp.bfloat16


def iota(shape, dim):
    return lax.broadcasted_iota(jnp.int32, shape, dim)


def dot_nt(a, b):
    return lax.dot_general(a, b, (((1,), (1,)), ((), ())), preferred_element_type=F32)


def dot_nn(a, b):
    return lax.dot_general(a, b, (((1,), (0,)), ((), ())), preferred_element_type=F32)


PIECES = 1


def pack_kernel(loc_hbm, valid_hbm, x_hbm, o_ref, loc_ref, valid_ref, x_ref, sems):
    count = x_ref.shape[0]
    size = count // PIECES
    copies = [
        pltpu.make_async_copy(x_hbm.at[pl.ds(i * size, size)], x_ref.at[pl.ds(i * size, size)], sems.at[i])
        for i in range(PIECES)
    ]
    small = [
        pltpu.make_async_copy(loc_hbm, loc_ref, sems.at[PIECES]),
        pltpu.make_async_copy(valid_hbm, valid_ref, sems.at[PIECES + 1]),
    ]
    for copy in small + copies:
        copy.start()
    for copy in small:
        copy.wait()
    row = iota((128, 128), 0)
    col = iota((128, 128), 1)
    valid = jnp.broadcast_to(valid_ref[...].astype(F32), (128, 128))
    pick = jnp.where(col == 16 * (row % 8) + row // 8, valid, 0.0).astype(BF16)
    jit = jnp.broadcast_to((loc_ref[...] & 1).astype(F32), (16, 128))
    jit = jnp.where(iota((16, 128), 1) // 16 == iota((16, 128), 0), jit, 0.0).astype(BF16)
    spread = jnp.where(col == row % 16, 1.0, 0.0).astype(BF16)
    bits = dot_nn(jit, spread)[0:8].astype(BF16)
    for i, copy in enumerate(copies):
        copy.wait()
        for g in range(i * size, (i + 1) * size):
            o_ref[g, 0:128] = dot_nt(pick, x_ref[g]).astype(BF16)
            o_ref[g, 128:136] = bits


def pack(channel_loc, channel_valid, blocks):
    count = blocks.shape[0]
    return pl.pallas_call(
        pack_kernel,
        in_specs=[pl.BlockSpec(memory_space=pl.ANY)] * 3,
        out_specs=pl.BlockSpec(memory_space=pltpu.VMEM),
        out_shape=pltpu.VMEM((count, 136, 128), BF16),
        scratch_shapes=[
            pltpu.VMEM((1, 128), jnp.int32),
            pltpu.VMEM((1, 128), jnp.int32),
            pltpu.VMEM((count, 128, 128), BF16),
            pltpu.SemaphoreType.DMA((PIECES + 2,)),
        ],
        name="pack",
    )(channel_loc.reshape(1, 128), channel_valid.reshape(1, 128), blocks)


def split3(x):
    hi = x.astype(BF16)
    rest = x - hi.astype(F32)
    mid = rest.astype(BF16)
    low = (rest - mid.astype(F32)).astype(BF16)
    return hi, mid, low


def skew_sum(x):
    total = x[0:8]
    for g in range(1, 16):
        total = total + pltpu.roll(x[8 * g : 8 * g + 8], 128 - 8 * g, 1)
    out = total[0:1]
    for s in range(1, 8):
        out = out + pltpu.roll(total[s : s + 1], 128 - s, 1)
    return out


def exact_dot(x, picks):
    hi, mid, rest = split3(x)
    return dot_nn(hi, picks) + dot_nn(mid, picks) + dot_nn(rest, picks)


CHUNK = 32
NCHUNK = 128 // CHUNK


def main_kernel(owner_hbm, y_ref, o_ref, owner_row_ref, sem, x_s, w_s, lin_s, mask_s, lin_acc, acc_s, pw_s):
    copy = pltpu.make_async_copy(owner_hbm, owner_row_ref, sem)
    copy.start()
    lane = iota((128, 128), 1)
    row = iota((128, 128), 0)
    sign = jnp.where(row // 32 % 2 == 1, 1.0, -1.0)
    swap = jnp.where(row == jnp.where(lane // 32 % 2 == 0, lane + 32, lane - 32), sign, 0.0).astype(BF16)
    bits_t = y_ref[:, 128:136, :].astype(F32).reshape(128, 128)
    bits = jnp.transpose(bits_t)
    own = [jnp.where(lane // 64 == f, 1.0, 0.0).astype(BF16) for f in range(2)]

    edge = jnp.where(row > lane, 1.0, jnp.where(row < lane, 0.0, -1.0))
    suffix = jnp.zeros((128, 128), F32)
    for r in reversed(range(16)):
        late = jnp.broadcast_to(bits_t[:, r : r + 1], (128, 128))
        gap = late - jnp.broadcast_to(bits[r : r + 1, :], (128, 128))
        mask_s[r] = jnp.minimum(jnp.maximum(edge + gap, 0.0), 1.0)
        x = y_ref[:, 8 * r : 8 * r + 8, :].astype(F32).reshape(128, 128)
        xb = x.astype(BF16)
        w_s[r, 0:128, :] = xb
        w_s[r, 128:256, :] = dot_nn(xb, swap).astype(BF16)
        hi = suffix.astype(BF16)
        low = (suffix - hi.astype(F32)).astype(BF16)
        for f in range(2):
            mine = xb * own[f]
            for c in range(NCHUNK):
                x_s[f, c, CHUNK * r : CHUNK * r + CHUNK, :] = mine[CHUNK * c : CHUNK * c + CHUNK]
            lin_s[f, r, 0] = hi * own[f]
            lin_s[f, r, 1] = low * own[f]
        suffix = suffix + x

    acc_s[...] = jnp.zeros(acc_s.shape, F32)

    keep_diag = row >= lane

    def one_freq(f):
        lin = jnp.zeros((128, 256), F32)
        lin_acc[f] = jnp.zeros((128, 256), F32)
        for r in reversed(range(16)):
            w = w_s[r]
            lin = lin + dot_nt(jnp.concatenate([lin_s[f, r, 0], lin_s[f, r, 1]], 1), jnp.concatenate([w, w], 1))
            for c in range(NCHUNK):
                rows = slice(CHUNK * c, CHUNK * c + CHUNK)
                prod = dot_nt(x_s[f, c, CHUNK * r :, :], w)
                mask = mask_s[r, rows]
                for u in range(r, 16):
                    at = CHUNK * (u - r)
                    re = prod[at : at + CHUNK, 0:128]
                    im = prod[at : at + CHUNK, 128:256]
                    gain = lax.rsqrt(jnp.maximum(re * re + im * im, 1.0))
                    if u == r:
                        lin_acc[f, rows, 0:128] += re * mask
                        lin_acc[f, rows, 128:256] += im * mask
                        gain = gain * mask
                        acc_re = re * gain
                        acc_im = im * gain
                    else:
                        acc_re = acc_re + re * gain
                        acc_im = acc_im + im * gain
                acc_s[f, rows, 0:128] += acc_re
                acc_s[f, rows, 128:256] += acc_im
        for part in range(4):
            cols = slice(128 * (part % 2), 128 * (part % 2) + 128)
            full = lin[:, cols] + lin_acc[f, :, cols] if part < 2 else acc_s[f, :, cols]
            low = skew_sum(jnp.where(keep_diag, full, 0.0))
            up = skew_sum(jnp.where(keep_diag, 0.0, full))
            pw_s[f, part : part + 1, 0:128] = low
            pw_s[f, part : part + 1, 128:256] = up if part % 2 == 0 else -up

    pw_s[...] = jnp.zeros(pw_s.shape, F32)
    for f in range(2):
        one_freq(f)

    low_pick = jnp.where((lane + row) % 128 == 0, 1.0, 0.0)
    up_pick = jnp.where(row == lane + 1, 1.0, 0.0)
    unpick = jnp.concatenate([low_pick, up_pick], 0).astype(BF16)
    sums = exact_dot(pw_s[...].reshape(16, 256), unpick)
    out = []
    for f in range(2):
        part = [sums[8 * f + p : 8 * f + p + 1] for p in range(4)]
        power = part[2] * part[2] + part[3] * part[3]
        out += [part[0], part[1], part[0] * power, part[1] * power]
    copy.wait()
    owner_row = jnp.broadcast_to(owner_row_ref[...], (128, 128))
    earlier = (owner_row == jnp.transpose(owner_row)) & (row < lane)
    rank = jnp.sum(jnp.where(earlier, 1.0, 0.0), 0, keepdims=True).astype(jnp.int32)
    slot = 16 * owner_row_ref[...] + rank
    place = jnp.where(iota((256, 128), 0) == slot, 1.0, 0.0).astype(BF16)
    by_bin = jnp.transpose(jnp.concatenate(out + [jnp.zeros((120, 128), F32)], 0))
    hi, mid, rest = split3(by_bin)
    placed = dot_nn(place, hi) + dot_nn(place, mid) + dot_nn(place, rest)
    o_ref[...] = placed[:, 0:8]


def bin_sums(bin_owner, received):
    vmem = pl.BlockSpec(memory_space=pltpu.VMEM)
    return pl.pallas_call(
        main_kernel,
        in_specs=[pl.BlockSpec(memory_space=pl.ANY), vmem],
        out_specs=vmem,
        out_shape=pltpu.VMEM((256, 8), F32),
        scratch_shapes=[
            pltpu.VMEM((1, 128), jnp.int32),
            pltpu.SemaphoreType.DMA(()),
            pltpu.VMEM((2, NCHUNK, 16 * CHUNK, 128), BF16),
            pltpu.VMEM((16, 256, 128), BF16),
            pltpu.VMEM((2, 16, 2, 128, 128), BF16),
            pltpu.VMEM((16, 128, 128), F32),
            pltpu.VMEM((2, 128, 256), F32),
            pltpu.VMEM((2, 128, 256), F32),
            pltpu.VMEM((2, 8, 256), F32),
        ],
        name="bin_sums",
    )(bin_owner.reshape(1, 128), received)


def lag_tables():
    lane = np.arange(128)
    f0 = lane // 8 * 2 + lane % 8 // 4
    imag = lane % 2
    weight = np.full((16, 128), 2.0) * np.where(f0 % 2, -1.0, 1.0)
    weight[0, f0 == 0] = 1.0
    turn0 = 2 * np.pi * (np.arange(32)[:, None] * np.arange(16) % 32) / 32
    first = np.concatenate([np.cos(turn0), np.sin(turn0)], 0)
    turn1 = 2 * np.pi * (np.arange(128)[:, None] * f0 % 1024) / 1024
    t1 = np.where(imag, -np.sin(turn1), np.cos(turn1))
    t2 = np.where(imag, -np.cos(turn1), -np.sin(turn1))
    turn2 = 2 * np.pi * (np.arange(8)[:, None] * f0 % 8) / 8
    which = [lane % 4 // 2 == 0, lane % 4 // 2 == 1]
    last = [np.concatenate([np.cos(turn2) * w, -np.sin(turn2) * w], 1) for w in which]
    return [np.asarray(t, np.float32) for t in (weight, first, np.stack([t1, t2]), np.concatenate(last, 0))]


def dot3(a, b, dim):
    ah = a.astype(BF16)
    al = (a - ah.astype(F32)).astype(BF16)
    bh = b.astype(BF16)
    bl = (b - bh.astype(F32)).astype(BF16)
    dot = dot_nt if dim else dot_nn
    return dot(ah, bh) + (dot(ah, bl) + dot(al, bh))


def finish_kernel(x_ref, weight_ref, first_ref, twiddle_ref, last_ref, lin_ref, phase_ref):
    spread = jnp.where(iota((8, 128), 0) == iota((8, 128), 1) % 8, 1.0, 0.0).astype(BF16)
    wide = exact_dot(x_ref[...], spread)
    wide = jnp.where(iota((256, 128), 0) % 16 == iota((256, 128), 1) // 8, wide, 0.0)
    z = jnp.sum(wide.reshape(16, 16, 128), 1) * weight_ref[...]
    v = dot3(first_ref[...], z, 0)
    g = jnp.concatenate([v[0:32]] * 4, 0)
    h = jnp.concatenate([v[32:64]] * 4, 0)
    t1 = twiddle_ref[0]
    t2 = twiddle_ref[1]
    q = jnp.concatenate([g * t1 + h * t2, h * t1 - g * t2], 1)
    series = dot3(last_ref[...], q, 1)
    for i, o_ref in enumerate((lin_ref, phase_ref)):
        c = series[8 * i : 8 * i + 8]
        o_ref[...] = c / jnp.sqrt(jnp.sum(c * c) * (1.0 / 1024) + 1e-06)


def finish(mine):
    vmem = pl.BlockSpec(memory_space=pltpu.VMEM)
    return pl.pallas_call(
        finish_kernel,
        in_specs=[vmem] * 5,
        out_specs=[vmem] * 2,
        out_shape=[jax.ShapeDtypeStruct((8, 128), F32)] * 2,
        name="finish",
    )(mine, *[in_vmem(jnp.asarray(t)) for t in lag_tables()])


def in_vmem(x):
    return pltpu.with_memory_space_constraint(x, pltpu.VMEM)


def exchange(x, axis):
    return lax.all_to_all(x, axis, split_axis=0, concat_axis=0, tiled=True)


def on_device(spectra, channel_loc, channel_valid, bin_owner):
    blocks = spectra.reshape(lax.axis_size("loop"), 128, 128)
    received = exchange(pack(channel_loc, channel_valid, blocks), "loop")
    received = in_vmem(received)
    sums = bin_sums(bin_owner, received)
    linear, phase = finish(in_vmem(exchange(sums, ("stack", "loop"))))
    return linear.reshape(1, 1, -1), phase.reshape(1, 1, -1)


def solution(mesh):
    in_specs = (P("stack", None, None, "loop"), P("loop"), P("loop"), P())
    out_specs = (P("stack", "loop", None), P("stack", "loop", None))
    return jax.shard_map(
        on_device, mesh=mesh, in_specs=in_specs, out_specs=out_specs, check_vma=False
    )
```
